32 devices in a mesh: seq: 8 (over z, y), batch: 4 (over x, core).
Axes of the slice: x: 2, y: 2, z: 4, core: 2. Of those that a mesh axis runs over, the one named last changes fastest.
Arguments:
- signal: bfloat16 [4, 1024, 8192], P('batch', 'seq'), may hold values from -6 to 6
- out_grad: bfloat16 [4, 1024, 8192], P('batch', 'seq'), may hold values from -6 to 6
- residues: float32 [8, 8192], replicated, may hold values from -0.3 to 0.3
- log_rates: float32 [8, 512], replicated, as said below
Outputs:
- mixed: bfloat16 [4, 1024, 8192], P('batch', 'seq')
- grad_signal: bfloat16 [4, 1024, 8192], P('batch', 'seq')
- grad_residues: float32 [8, 8192], replicated
- grad_rates: float32 [8, 512], replicated
The draws below stay inside these ranges and needn't reach their ends.
Inputs may be any that keep to these rules, and one draw needn't show every extreme that they name: Each decay rate exp(log_rates) lies between 0.2 / 1024 and 1 / 30.
All inputs are finite; a program needn't handle non-finite values.
Results may differ from the reference program's by a relative error of at most 0.0012.
Values sent between devices are 32-bit elements; how exact they have to be, the bound alone decides.
A program may use at most 384 MiB of HBM per device.

```python
import jax
import jax.numpy as jnp
from jax import lax

D = 8192
M = 8
GROUP = 16
LEN = 1024
BATCH = 4


def draw_log_rates(key, part):
    key_coin, key_slow, key_fast = jax.random.split(key, 3)
    shape = (M, D // GROUP)
    slow_share = 0.125
    coin = jax.random.uniform(key_coin, shape, jnp.float32) < slow_share
    slow_low = jnp.log(0.2 / LEN)
    slow_high = jnp.log(2.0 / LEN)
    fast_low = jnp.log(0.01)
    fast_high = jnp.log(1.0 / 30.0)
    slow_value = slow_low + jax.random.uniform(key_slow, shape, jnp.float32) * (slow_high - slow_low)
    fast_value = fast_low + jax.random.uniform(key_fast, shape, jnp.float32) * (fast_high - fast_low)
    return jnp.where(coin, slow_value, fast_value).astype(jnp.float32)


def steps_of(rng, shape, shards, smallest, high):
    def one(position, blocks):
        draws = jax.random.uniform(jax.random.fold_in(jax.random.fold_in(rng, 6), position), (blocks,), jnp.float32, smallest / len(shards), high / len(shards))
        return jnp.repeat(jnp.exp(draws), shape[position] // blocks).reshape((-1,) + (1,) * (len(shape) - position - 1))

    loudness = one(*shards[0])
    for cut in shards[1:]:
        loudness = loudness * one(*cut)
    return loudness


def normal_values(key, extent, scale, most, cuts=(), held_as=jnp.bfloat16):
    drawn = scale * jax.random.normal(key, extent, jnp.float32)
    if cuts:
        drawn = drawn * steps_of(key, extent, cuts, -0.22, 0.18)
    return jnp.clip(drawn, -most, most).astype(held_as)


def setup_inputs(seed: int = 0) -> dict:
    splits = jax.random.split(jax.random.key(seed), 5)
    signal = normal_values(splits[0], (BATCH, LEN, D), 1.0, 6.0, ((0, 4), (1, 8)))
    out_grad = normal_values(splits[1], (BATCH, LEN, D), 1.0, 6.0, ((0, 4), (1, 8)))
    residues = normal_values(splits[2], (M, D), 0.05, 0.3, (), jnp.float32)
    log_rates = draw_log_rates(jax.random.fold_in(splits[4], 71), 0)
    return dict(signal=signal, out_grad=out_grad, residues=residues, log_rates=log_rates)


def expand(values):
    return jnp.repeat(values, GROUP, axis=1)


def reference(signal, out_grad, residues, log_rates):
    decay_rate = jnp.exp(log_rates)
    pole_values = expand(jnp.exp(-decay_rate))
    empty_state = jnp.zeros((BATCH, M, D), jnp.float32)
    empty_sum = jnp.zeros((M, D), jnp.float32)

    def forward_step(carried, rows):
        modal_state, moment, sum_residue, sum_moment = carried
        signal_row = rows[0].astype(jnp.float32)[:, None, :]
        grad_row = rows[1].astype(jnp.float32)[:, None, :]
        moment = pole_values * (moment + modal_state)
        modal_state = pole_values * modal_state + signal_row
        out_row = jnp.sum(residues * modal_state, axis=1)
        sum_residue = sum_residue + jnp.sum(grad_row * modal_state, axis=0)
        sum_moment = sum_moment + jnp.sum(grad_row * moment, axis=0)
        return (modal_state, moment, sum_residue, sum_moment), out_row.astype(jnp.bfloat16)

    rows = (jnp.swapaxes(signal, 0, 1), jnp.swapaxes(out_grad, 0, 1))
    finals, outputs = lax.scan(forward_step, (empty_state, empty_state, empty_sum, empty_sum), rows)

    def backward_step(adjoint, grad_in):
        adjoint = pole_values * adjoint + grad_in.astype(jnp.float32)[:, None, :]
        return adjoint, jnp.sum(residues * adjoint, axis=1).astype(jnp.bfloat16)

    unused, grads = lax.scan(backward_step, empty_state, rows[1], reverse=True)
    norm_factor = 1.0 / (BATCH * LEN)
    grad_residues = finals[2] * norm_factor
    grad_rates = -decay_rate * jnp.sum((residues * finals[3]).reshape(M, D // GROUP, GROUP), axis=2) * norm_factor
    return jnp.swapaxes(outputs, 0, 1), jnp.swapaxes(grads, 0, 1), grad_residues, grad_rates
```

```python
import functools

import jax
import jax.numpy as jnp
import numpy as np
from jax import lax
from jax.experimental import pallas as pl
from jax.experimental.pallas import tpu as pltpu
from jax.sharding import PartitionSpec as P

LANES = 256
TILE = 128
SUB = 4
F32 = jnp.float32
BF16 = jnp.bfloat16
MESH = pl.DeviceIdType.MESH


def split(value):
    high = value.astype(BF16)
    return high, (value - high.astype(F32)).astype(BF16)


def mul(a, b):
    return jnp.dot(a, b, preferred_element_type=F32)


def twice(value, axis):
    return jnp.concatenate([value, value], axis=axis)


def own_rows(wide, modes, group):
    rows, lanes = wide.shape
    owner = lax.broadcasted_iota(jnp.int32, (modes, lanes), 1) // group
    out = wide[:modes]
    for g in range(1, rows // modes):
        out = jnp.where(owner == g, wide[g * modes : (g + 1) * modes], out)
    return out


def spread(narrow, rows, group):
    modes, lanes = narrow.shape
    owner = lax.broadcasted_iota(jnp.int32, (modes, lanes), 1) // group
    return jnp.concatenate(
        [jnp.where(owner == g, narrow, 0.0) for g in range(rows // modes)], axis=0
    )


def pick_lanes(tile, index):
    return jnp.take_along_axis(tile, index, axis=1, mode="promise_in_bounds")


def state_block(modes, group, rate, x, g):
    rows, length = rate.shape
    at = lax.broadcasted_iota(jnp.int32, (rows, length), 1).astype(F32)
    rising = jnp.exp(-rate * at)
    falling = jnp.exp(-rate * (length - 1.0 - at))
    out = []
    for table, weight, values in ((falling, length - at, x), (rising, at, g)):
        left = jnp.concatenate([table, weight * table], axis=0)
        both = mul(jnp.concatenate(split(left), axis=1), twice(values, 0))
        out.append((own_rows(both[:rows], modes, group), own_rows(both[rows:], modes, group)))
    return out


def phi_of(rate, angle):
    pole = jnp.exp(-rate)
    gap = jnp.ones_like(rate)
    for k in range(7, 1, -1):
        gap = 1.0 - rate * gap * (1.0 / k)
    gap = rate * gap
    real = gap + pole * angle[0]
    imag = pole * angle[1]
    inverse = 1.0 / (real * real + imag * imag)
    return real * inverse, -imag * inverse


def lag_block(modes, group, rate, dft, angle, x, g):
    half = x.shape[0] // 2
    gm = rate.shape[1]
    phi_r, phi_i = phi_of(rate, angle)
    psi_r = phi_r * phi_r - phi_i * phi_i - phi_r
    psi_i = 2.0 * phi_r * phi_i - phi_i
    phi_t = jnp.concatenate([phi_r, -phi_i], axis=0).T
    psi_t = jnp.concatenate([psi_r, -psi_i], axis=0).T
    x_hat = mul(dft, twice(x, 0))
    g_hat = mul(dft, twice(g, 0))
    xr, xi = x_hat[:half], x_hat[half:]
    gr, gi = g_hat[:half], g_hat[half:]
    lag = jnp.concatenate([gr * xr + gi * xi, gr * xi - gi * xr], axis=0) * (1.0 / half)
    terms_high, terms_low = split(jnp.concatenate([phi_t, psi_t], axis=0))
    lag_high, lag_low = split(lag)
    wide = mul(jnp.concatenate([terms_high, terms_low], 1), twice(lag_high, 0)) + mul(
        terms_high, lag_low
    )
    return x_hat, g_hat, own_rows(wide[:gm], modes, group), own_rows(wide[gm:], modes, group)


def out_block(group, rate, inv_high, inv_low, angle, x_hat, g_hat, res, start_x, start_g):
    length = x_hat.shape[0]
    half = length // 2
    gm = rate.shape[1]
    phi_r, phi_i = phi_of(rate, angle)
    phi_high, phi_low = split(jnp.concatenate([phi_r, phi_i], axis=0))
    res_high, res_low = split(spread(res, gm, group))
    k_hat = mul(jnp.concatenate([phi_high, phi_low], 1), twice(res_high, 0)) + mul(phi_high, res_low)
    xr, xi = x_hat[:half], x_hat[half:]
    gr, gi = g_hat[:half], g_hat[half:]
    kr, ki = k_hat[:half], k_hat[half:]
    y_hat = jnp.concatenate([kr * xr - ki * xi, kr * xi + ki * xr], axis=0)
    h_hat = jnp.concatenate([kr * gr + ki * gi, kr * gi - ki * gr], axis=0)
    when = lax.broadcasted_iota(jnp.int32, (length, gm), 0).astype(F32)
    rising = jnp.exp(-rate * (when + 1.0))
    falling = jnp.exp(-rate * (length - when))
    outs = []
    for hat, table, start in ((y_hat, rising, start_x), (h_hat, falling, start_g)):
        hat_high, hat_low = split(hat)
        table_high, table_low = split(table)
        start_high, start_low = split(spread(start, gm, group))
        outs.append(
            mul(jnp.concatenate([inv_high, inv_low], 1), twice(hat_high, 0))
            + mul(jnp.concatenate([table_high, table_low], 1), twice(start_high, 0))
            + mul(
                jnp.concatenate([inv_high, table_high], 1),
                jnp.concatenate([hat_low, start_low], 0),
            )
        )
    return outs


def remote(source, target, sems, k, where):
    return pltpu.make_async_remote_copy(
        src_ref=source, dst_ref=target, send_sem=sems[0].at[k], recv_sem=sems[1].at[k],
        device_id=where, device_id_type=MESH,
    )


def whole_kernel(
    n, rows, norm, modes, group, owners, plan,
    x_hbm, g_hbm, res_hbm, log_hbm, dft_ref, inv_high_ref, inv_low_ref, angle_ref,
    y_hbm, gs_hbm, gres_ref, grate_ref,
    x_ref, g_ref, res_ref, log_ref, y_ref, gs_ref, decay_ref, rates_ref, rows_ref,
    state_ref, weighted_ref, x_hat_ref, g_hat_ref, sum_ref, moment_ref,
    pair_ref, total_ref, outer_ref, back_ref, landed_ref, sum_pair_ref, owned_ref,
    reduced_ref, gathered_ref, rate_ref, rate_row_ref, rate_seq_ref,
    in_sems, out_sems, *sems,
):
    length, channels = x_ref.shape
    groups = log_ref.shape[1]
    half = channels // 2
    chunk = SUB * LANES
    count = half // chunk
    steps = 2 * count
    outer = n // 2
    me = lax.axis_index("seq")
    mine = lax.axis_index("batch")
    z, side = lax.div(me, 2), lax.rem(me, 2)
    own_base, pair_base = side * half, (1 - side) * half
    unit = half // (rows * owners)
    pairs = [(sems[2 * i], sems[2 * i + 1]) for i in range(len(sems) // 2)]
    partner = {"seq": me + 1 - 2 * side}

    def lanes(start, width=chunk):
        return pl.ds(pl.multiple_of(start, TILE), width)

    def base_of(j):
        return jnp.where(j < count, pair_base + j * chunk, own_base + (j - count) * chunk)

    def loads(j):
        here = lanes(base_of(j))
        return [
            pltpu.make_async_copy(x_hbm.at[:, here], x_ref.at[:, here], in_sems.at[j]),
            pltpu.make_async_copy(g_hbm.at[:, here], g_ref.at[:, here], in_sems.at[steps + j]),
        ]

    load_log = pltpu.make_async_copy(log_hbm, log_ref, in_sems.at[2 * steps])
    load_res = pltpu.make_async_copy(res_hbm, res_ref, in_sems.at[2 * steps + 1])

    def stores(j, base):
        here = lanes(base)
        return [
            pltpu.make_async_copy(y_ref.at[:, here], y_hbm.at[:, here], out_sems.at[j]),
            pltpu.make_async_copy(gs_ref.at[:, here], gs_hbm.at[:, here], out_sems.at[steps + j]),
        ]

    def to_pair(k):
        here = lanes(pair_base + k * chunk)
        return remote(
            state_ref.at[:, :, here], pair_ref.at[:, :, lanes(k * chunk)], pairs[0], k, partner
        )

    def to_outer(k):
        out = []
        for i in range(1, outer):
            peer = lax.rem(z + i, outer)
            here = lanes(k * chunk)
            out.append(
                remote(
                    total_ref.at[jnp.where(peer > z, 0, 1), :, here], outer_ref.at[z, :, here],
                    pairs[1], (i - 1) * count + k, {"seq": 2 * peer + side},
                )
            )
        return out

    def to_back(k):
        return remote(
            back_ref.at[:, :, lanes(k * chunk)], landed_ref.at[:, :, lanes(own_base + k * chunk)],
            pairs[2], k, partner,
        )

    def sums_to_pair():
        return remote(sum_ref.at[:, lanes(pair_base, half)], sum_pair_ref, pairs[3], 0, partner)

    def owned_at(q, zo):
        return q * (half // rows) + zo * unit

    def guarded(condition, action):
        if owners == outer:
            action()
        else:
            pl.when(condition)(action)

    near = [(q, i) for q in range(rows) for i in range(outer) if q or i]
    far = [(q, i) for q in range(rows) for i in range(n) if q or i]

    def reduce_copy(k):
        q, i = near[k]
        peer_q, peer_z = lax.rem(mine + q, rows), lax.rem(z + i, outer)
        return peer_z, remote(
            owned_ref.at[:, lanes(owned_at(peer_q, jnp.minimum(peer_z, owners - 1)), unit)],
            reduced_ref.at[k], pairs[4], k, {"batch": peer_q, "seq": 2 * peer_z + side},
        )

    def gather_copy(k):
        q, i = far[k]
        here = lanes(own_base + owned_at(mine, jnp.minimum(z, owners - 1)), unit)
        return lax.div(lax.rem(me + n - i, n), 2), remote(
            gathered_ref.at[:, here], gathered_ref.at[:, here], pairs[5], k,
            {"batch": lax.rem(mine + q, rows), "seq": lax.rem(me + i, n)},
        )

    def rates_beside():
        return [
            remote(
                rate_row_ref.at[mine], rate_row_ref.at[mine], pairs[6], i - 1,
                {"batch": lax.rem(mine + i, rows)},
            )
            for i in range(1, rows)
        ]

    def rates_along():
        return [
            remote(
                rate_seq_ref.at[me], rate_seq_ref.at[me], pairs[7], i - 1,
                {"seq": lax.rem(me + i, n)},
            )
            for i in range(1, n)
        ]

    load_log.start()
    barrier = pltpu.get_barrier_semaphore()
    for copy in loads(0):
        copy.start()
    for q, i in far:
        pl.semaphore_signal(
            barrier, inc=1, device_id={"batch": lax.rem(mine + q, rows), "seq": lax.rem(me + i, n)},
            device_id_type=MESH,
        )
    for j in range(1, steps):
        for copy in loads(j):
            copy.start()
    load_res.start()
    outer_ref[z] = jnp.zeros((modes, half), F32)

    load_log.wait()
    decay_ref[...] = jnp.exp(log_ref[...])
    lane = lax.broadcasted_iota(jnp.int32, (modes, TILE), 1)
    sub = lax.broadcasted_iota(jnp.int32, (modes, TILE), 0)
    per_tile = TILE // group
    for k in range(channels // TILE):
        first = k * per_tile
        tile = decay_ref[:, first // TILE * TILE : (first // TILE + 1) * TILE]
        rates_ref[:, k * TILE : (k + 1) * TILE] = pick_lanes(tile, lane // group + first % TILE)
    per_block = LANES // group
    for b in range(channels // LANES):
        first = b * per_block
        tile = decay_ref[:, first // TILE * TILE : (first // TILE + 1) * TILE]
        taken = pick_lanes(tile, lane // modes + first % TILE)
        row = jnp.sum(jnp.where(lane % modes == sub, taken, 0.0), axis=0, keepdims=True)
        rows_ref[b] = jnp.broadcast_to(row, (modes, TILE))

    def states(j, nothing):
        base = base_of(j)
        for copy in loads(j):
            copy.wait()
        for s in range(SUB):
            at = lanes(base + s * LANES, LANES)
            first = lax.div(base, group) + s * per_block
            tile = decay_ref[:, lanes(lax.div(first, TILE) * TILE, TILE)]
            shift = lax.rem(first, TILE)
            rate = jnp.concatenate(
                [pick_lanes(tile, jnp.full((modes, TILE), shift + g)) for g in range(per_block)], 0
            )
            (s_x, w_x), (s_g, w_g) = state_block(modes, group, rate, x_ref[:, at], g_ref[:, at])
            state_ref[0, :, at] = s_x
            state_ref[1, :, at] = s_g
            weighted_ref[0, :, at] = w_x
            weighted_ref[1, :, at] = w_g

        for k in range(count):
            @pl.when(j == k)
            def _():
                if k == 0:
                    pl.semaphore_wait(barrier, len(far))
                to_pair(k).start()

        return nothing

    lax.fori_loop(0, steps, states, 0)

    def both_of(k):
        at, here = lanes(own_base + k * chunk), lanes(k * chunk)
        first = side == 0
        ours, theirs = [state_ref[i, :, at] for i in (0, 1)], [pair_ref[i, :, here] for i in (0, 1)]
        a = [jnp.where(first, o, t) for o, t in zip(ours, theirs)]
        b = [jnp.where(first, t, o) for o, t in zip(ours, theirs)]
        return a, b, jnp.exp(-rates_ref[:, at] * float(length)), first, at, here

    def send_total(k):
        to_pair(k).wait_recv()
        a, b, whole, first, at, here = both_of(k)
        total_ref[0, :, here] = whole * a[0] + b[0]
        total_ref[1, :, here] = a[1] + whole * b[1]
        for copy in to_outer(k):
            copy.start()

    def take_total(k):
        for copy in to_outer(k):
            copy.wait_recv()
        a, b, whole, first, at, here = both_of(k)
        twofold = whole * whole
        carry = jnp.zeros_like(whole)
        adjoint = jnp.zeros_like(whole)
        for i in range(outer):
            carry = jnp.where(i < z, outer_ref[i, :, here] + twofold * carry, carry)
            last = outer - 1 - i
            adjoint = jnp.where(last > z, outer_ref[last, :, here] + twofold * adjoint, adjoint)
        carry_b = whole * carry + a[0]
        adjoint_a = whole * adjoint + b[1]
        back_ref[0, :, here] = jnp.where(first, carry_b, carry)
        back_ref[1, :, here] = jnp.where(first, adjoint, adjoint_a)
        to_back(k).start()
        landed_ref[0, :, at] = jnp.where(first, carry, carry_b)
        landed_ref[1, :, at] = jnp.where(first, adjoint_a, adjoint)
        fold = 1.0 / (1.0 + whole)
        cross = (carry + a[0] * fold) * a[1] + (carry_b + b[0] * fold) * b[1]
        owned_ref[:, here] = jnp.exp(-rates_ref[:, at]) * cross

    def start_reduce():
        sums_to_pair().wait_recv()
        owned_ref[...] = owned_ref[...] + (sum_ref[:, lanes(own_base, half)] + sum_pair_ref[...])
        for k in range(len(near)):
            peer_z, copy = reduce_copy(k)
            guarded(peer_z < owners, copy.start)

    def start_rates():
        many = TILE // per_block
        row_id = lax.broadcasted_iota(jnp.int32, (LANES, TILE), 0) // group
        col_id = lax.broadcasted_iota(jnp.int32, (LANES, TILE), 1)

        def lap(c, nothing):
            added = jnp.zeros((2 * modes, TILE), F32)
            for j in range(many):
                at = lanes((c * many + j) * LANES, LANES)
                rate = rates_ref[:, at]
                pole = jnp.exp(-rate)
                whole = jnp.exp(-rate * float(length))
                fold = 1.0 / (1.0 + whole)
                turned_x, turned_g = state_ref[0, :, at] * fold, state_ref[1, :, at] * fold
                carry, adjoint = landed_ref[0, :, at], landed_ref[1, :, at]
                carry_all, adjoint_all = carry + turned_x, adjoint + turned_g
                moments = (
                    moment_ref[:, at]
                    + pole * (carry_all * weighted_ref[1, :, at] + adjoint_all * weighted_ref[0, :, at])
                    + float(length) * pole * whole * (carry * adjoint - turned_x * turned_g)
                )
                pick = jnp.where(row_id + j * per_block == col_id, 1.0, 0.0).astype(BF16)
                added += mul(jnp.concatenate(split(-rate * res_ref[:, at] * moments), 0), pick)
            rate_row_ref[mine, :, lanes(c * TILE, TILE)] = added[:modes] + added[modes:]
            return nothing

        lax.fori_loop(0, groups // TILE, lap, 0)
        for copy in rates_beside():
            copy.start()

    def lags(j, nothing):
        for k in range(count):
            @pl.when(j == plan["total"][k])
            def _():
                send_total(k)

        base = base_of(j)
        for s in range(SUB):
            at = lanes(base + s * LANES, LANES)
            rate = rows_ref[lax.div(base, LANES) + s, 0:1, :]
            x_hat, g_hat, sums, moments = lag_block(
                modes, group, rate, dft_ref[...], angle_ref[...], x_ref[:, at], g_ref[:, at]
            )
            x_hat_ref[:, at] = x_hat
            g_hat_ref[:, at] = g_hat
            sum_ref[:, at] = sums
            moment_ref[:, at] = moments

        @pl.when(j == count - 1)
        def _():
            sums_to_pair().start()

        for k in range(count):
            if plan["take"][k] < steps:
                @pl.when(j == plan["take"][k])
                def _():
                    take_total(k)

        return nothing

    lax.fori_loop(0, steps, lags, 0)
    load_res.wait()

    order = plan["order"]

    def base_out(j):
        base = own_base
        for i, (own, k) in enumerate(order):
            base = jnp.where(j == i, (own_base if own else pair_base) + k * chunk, base)
        return base

    def outs(j, nothing):
        for k in range(count):
            if plan["take"][k] >= steps:
                @pl.when(j == plan["take"][k] - steps)
                def _():
                    take_total(k)

        for i, (own, k) in enumerate(order):
            if not own:
                @pl.when(j == i)
                def _():
                    to_back(k).wait_recv()

        @pl.when(j == plan["reduce"])
        def _():
            start_reduce()

        @pl.when(j == plan["rates"])
        def _():
            start_rates()

        base = base_out(j)
        for s in range(SUB):
            at = lanes(base + s * LANES, LANES)
            rate = rows_ref[lax.div(base, LANES) + s, 0:1, :]
            res = res_ref[:, at]
            fold = 1.0 / (1.0 + jnp.exp(-rates_ref[:, at] * float(length)))
            start_x = res * (landed_ref[0, :, at] + state_ref[0, :, at] * fold)
            start_g = res * (landed_ref[1, :, at] + state_ref[1, :, at] * fold)
            y, gs = out_block(
                group, rate, inv_high_ref[...], inv_low_ref[...], angle_ref[...],
                x_hat_ref[:, at], g_hat_ref[:, at], res, start_x, start_g,
            )
            y_ref[:, at] = y.astype(BF16)
            gs_ref[:, at] = gs.astype(BF16)
        for copy in stores(j, base):
            copy.start()
        return nothing

    lax.fori_loop(0, steps, outs, 0)

    def finish_reduce():
        part = owned_ref[:, lanes(owned_at(mine, jnp.minimum(z, owners - 1)), unit)]
        for k in range(len(near)):
            reduce_copy(k)[1].wait_recv()
            part = part + reduced_ref[k]
        gathered_ref[:, lanes(own_base + owned_at(mine, jnp.minimum(z, owners - 1)), unit)] = part * norm
        for k in range(len(far)):
            gather_copy(k)[1].start()

    guarded(z < owners, finish_reduce)
    for copy in rates_beside():
        copy.wait_recv()
    part = rate_row_ref[0]
    for i in range(1, rows):
        part = part + rate_row_ref[i]
    rate_seq_ref[me] = part
    for copy in rates_along():
        copy.start()
    for copy in rates_along():
        copy.wait_recv()
    part = rate_seq_ref[0]
    for i in range(1, n):
        part = part + rate_seq_ref[i]
    grate_ref[...] = part * norm
    for k in range(len(far)):
        from_z, copy = gather_copy(k)
        guarded(from_z < owners, copy.wait_recv)
    gres_ref[...] = gathered_ref[...]

    for j in range(steps):
        for copy in stores(j, base_out(j)):
            copy.wait()
    for k in range(count):
        for copy in [to_pair(k), to_back(k)] + to_outer(k):
            copy.wait_send()
    sums_to_pair().wait_send()
    for k in range(len(near)):
        peer_z, copy = reduce_copy(k)
        guarded(peer_z < owners, copy.wait_send)
    for k in range(len(far)):
        guarded(z < owners, gather_copy(k)[1].wait_send)
    for copy in rates_beside() + rates_along():
        copy.wait_send()


def constants(length):
    half = length // 2
    omega = np.pi * (2.0 * np.arange(half) + 1.0) / length
    at = np.arange(length)
    forward = np.concatenate([np.cos(np.outer(omega, at)), -np.sin(np.outer(omega, at))], axis=0)
    lanes = np.ones((1, TILE))
    angle = np.stack(
        [2.0 * np.sin(omega / 2.0)[:, None] ** 2 * lanes, np.sin(omega)[:, None] * lanes]
    )
    return forward.astype(np.float32), (forward.T / half).astype(np.float32), angle.astype(np.float32)


def plan_of(count):
    own = [(True, k) for k in range(count)]
    pair = [(False, k) for k in range(count)]
    order = own[:2] + [v for both in zip(pair, own[2:] + [None] * 2) for v in both if v]
    return {
        "total": [min(2 * count - 1, k + 1) for k in range(count)],
        "take": [2 * count + order.index((True, k)) for k in range(count)],
        "order": order,
        "reduce": min(2 * count - 1, order.index((True, count - 1)) + 1),
        "rates": 2 * count - 1,
    }


def local(mesh_shape, signal, out_grad, residues, log_rates):
    batch_rows, length, channels = signal.shape
    modes, groups = log_rates.shape
    group = channels // groups
    n, rows = mesh_shape["seq"], mesh_shape["batch"]
    norm = 1.0 / (batch_rows * rows * length * n)
    forward, inverse, angle = constants(length)
    dft = np.asarray(forward).astype(jnp.bfloat16)
    dft = np.concatenate([dft, (forward - dft.astype(np.float32)).astype(jnp.bfloat16)], axis=1)
    inv_high = np.asarray(inverse).astype(jnp.bfloat16)
    inv_low = (inverse - inv_high.astype(np.float32)).astype(jnp.bfloat16)
    half = channels // 2
    outer = n // 2
    count = half // (SUB * LANES)
    steps = 2 * count
    owners = min(outer, half // (rows * TILE))
    unit = half // (rows * owners)

    def dma(size):
        return pltpu.SemaphoreType.DMA((max(size, 1),))

    def vmem(*shape, dtype=F32):
        return pltpu.VMEM(shape, dtype)

    any_spec = pl.BlockSpec(memory_space=pl.ANY)
    vmem_spec = pl.BlockSpec(memory_space=pltpu.VMEM)
    links = [count, (outer - 1) * count, count, 1, rows * outer - 1, rows * n - 1, rows - 1, n - 1]
    mixed, grads, res_sum, rate_sum = [], [], 0.0, 0.0
    for row in range(batch_rows):
        y, gs, part, rates = pl.pallas_call(
            functools.partial(whole_kernel, n, rows, norm, modes, group, owners, plan_of(count)),
            in_specs=[any_spec] * 4 + [vmem_spec] * 4,
            out_specs=[any_spec] * 2 + [vmem_spec] * 2,
            out_shape=[
                jax.ShapeDtypeStruct((length, channels), BF16),
                jax.ShapeDtypeStruct((length, channels), BF16),
                jax.ShapeDtypeStruct((modes, channels), F32),
                jax.ShapeDtypeStruct((modes, groups), F32),
            ],
            scratch_shapes=[
                vmem(length, channels, dtype=BF16),
                vmem(length, channels, dtype=BF16),
                vmem(modes, channels),
                vmem(modes, groups),
                vmem(length, channels, dtype=BF16),
                vmem(length, channels, dtype=BF16),
                vmem(modes, groups),
                vmem(modes, channels),
                vmem(channels // LANES, modes, TILE),
                vmem(2, modes, channels),
                vmem(2, modes, channels),
                vmem(length, channels),
                vmem(length, channels),
                vmem(modes, channels),
                vmem(modes, channels),
                vmem(2, modes, half),
                vmem(2, modes, half),
                vmem(outer, modes, half),
                vmem(2, modes, half),
                vmem(2, modes, channels),
                vmem(modes, half),
                vmem(modes, half),
                vmem(max(rows * outer - 1, 1), modes, unit),
                vmem(modes, channels),
                vmem(modes, groups),
                vmem(rows, modes, groups),
                vmem(n, modes, groups),
                dma(2 * steps + 2),
                dma(2 * steps),
            ]
            + [dma(size) for size in links for _ in range(2)],
            compiler_params=pltpu.CompilerParams(
                collective_id=0, has_side_effects=True, vmem_limit_bytes=48 * 1024 * 1024
            ),
        )(signal[row], out_grad[row], residues, log_rates, dft, inv_high, inv_low, angle)
        mixed.append(y)
        grads.append(gs)
        res_sum = res_sum + part if row else part
        rate_sum = rate_sum + rates if row else rates
    return jnp.stack(mixed), jnp.stack(grads), res_sum, rate_sum


def solution(mesh):
    placed = (P("batch", "seq", None), P("batch", "seq", None), P(), P())
    return jax.shard_map(
        functools.partial(local, dict(mesh.shape)),
        mesh=mesh,
        in_specs=placed,
        out_specs=placed,
        check_vma=False,
    )
```

```python
import functools

import jax
import jax.numpy as jnp
import numpy as np
from jax import lax
from jax.experimental import pallas as pl
from jax.experimental.pallas import tpu as pltpu
from jax.sharding import PartitionSpec as P

LANES = 256
TILE = 128
SUB = 4
F32 = jnp.float32
BF16 = jnp.bfloat16
MESH = pl.DeviceIdType.MESH


def split(value):
    high = value.astype(BF16)
    return high, (value - high.astype(F32)).astype(BF16)


def mul(a, b):
    return jnp.dot(a, b, preferred_element_type=F32)


def twice(value, axis):
    return jnp.concatenate([value, value], axis=axis)


def own_rows(wide, modes, group):
    rows, lanes = wide.shape
    owner = lax.broadcasted_iota(jnp.int32, (modes, lanes), 1) // group
    out = wide[:modes]
    for g in range(1, rows // modes):
        out = jnp.where(owner == g, wide[g * modes : (g + 1) * modes], out)
    return out


def spread(narrow, rows, group):
    modes, lanes = narrow.shape
    owner = lax.broadcasted_iota(jnp.int32, (modes, lanes), 1) // group
    return jnp.concatenate(
        [jnp.where(owner == g, narrow, 0.0) for g in range(rows // modes)], axis=0
    )


def pick_lanes(tile, index):
    return jnp.take_along_axis(tile, index, axis=1, mode="promise_in_bounds")


def state_block(modes, group, rate, x, g):
    rows, length = rate.shape
    at = lax.broadcasted_iota(jnp.int32, (rows, length), 1).astype(F32)
    rising = jnp.exp(-rate * at)
    falling = jnp.exp(-rate * (length - 1.0 - at))
    out = []
    for table, weight, values in ((falling, length - at, x), (rising, at, g)):
        left = jnp.concatenate([table, weight * table], axis=0)
        both = mul(jnp.concatenate(split(left), axis=1), twice(values, 0))
        out.append((own_rows(both[:rows], modes, group), own_rows(both[rows:], modes, group)))
    return out


def phi_of(rate, angle):
    pole = jnp.exp(-rate)
    gap = jnp.ones_like(rate)
    for k in range(7, 1, -1):
        gap = 1.0 - rate * gap * (1.0 / k)
    gap = rate * gap
    real = gap + pole * angle[0]
    imag = pole * angle[1]
    inverse = 1.0 / (real * real + imag * imag)
    return real * inverse, -imag * inverse


def lag_block(modes, group, rate, dft, angle, x, g):
    half = x.shape[0] // 2
    gm = rate.shape[1]
    phi_r, phi_i = phi_of(rate, angle)
    psi_r = phi_r * phi_r - phi_i * phi_i - phi_r
    psi_i = 2.0 * phi_r * phi_i - phi_i
    phi_t = jnp.concatenate([phi_r, -phi_i], axis=0).T
    psi_t = jnp.concatenate([psi_r, -psi_i], axis=0).T
    x_hat = mul(dft, twice(x, 0))
    g_hat = mul(dft, twice(g, 0))
    xr, xi = x_hat[:half], x_hat[half:]
    gr, gi = g_hat[:half], g_hat[half:]
    lag = jnp.concatenate([gr * xr + gi * xi, gr * xi - gi * xr], axis=0) * (1.0 / half)
    terms_high, terms_low = split(jnp.concatenate([phi_t, psi_t], axis=0))
    lag_high, lag_low = split(lag)
    wide = mul(jnp.concatenate([terms_high, terms_low], 1), twice(lag_high, 0)) + mul(
        terms_high, lag_low
    )
    return x_hat, g_hat, own_rows(wide[:gm], modes, group), own_rows(wide[gm:], modes, group)


def out_block(group, rate, inv_high, inv_low, angle, x_hat, g_hat, res, start_x, start_g):
    length = x_hat.shape[0]
    half = length // 2
    gm = rate.shape[1]
    phi_r, phi_i = phi_of(rate, angle)
    phi_high, phi_low = split(jnp.concatenate([phi_r, phi_i], axis=0))
    res_high, res_low = split(spread(res, gm, group))
    k_hat = mul(jnp.concatenate([phi_high, phi_low], 1), twice(res_high, 0)) + mul(phi_high, res_low)
    xr, xi = x_hat[:half], x_hat[half:]
    gr, gi = g_hat[:half], g_hat[half:]
    kr, ki = k_hat[:half], k_hat[half:]
    y_hat = jnp.concatenate([kr * xr - ki * xi, kr * xi + ki * xr], axis=0)
    h_hat = jnp.concatenate([kr * gr + ki * gi, kr * gi - ki * gr], axis=0)
    when = lax.broadcasted_iota(jnp.int32, (length, gm), 0).astype(F32)
    rising = jnp.exp(-rate * (when + 1.0))
    falling = jnp.exp(-rate * (length - when))
    outs = []
    for hat, table, start in ((y_hat, rising, start_x), (h_hat, falling, start_g)):
        hat_high, hat_low = split(hat)
        table_high, table_low = split(table)
        start_high, start_low = split(spread(start, gm, group))
        outs.append(
            mul(jnp.concatenate([inv_high, inv_low], 1), twice(hat_high, 0))
            + mul(jnp.concatenate([table_high, table_low], 1), twice(start_high, 0))
            + mul(
                jnp.concatenate([inv_high, table_high], 1),
                jnp.concatenate([hat_low, start_low], 0),
            )
        )
    return outs


def remote(source, target, sems, k, where):
    return pltpu.make_async_remote_copy(
        src_ref=source, dst_ref=target, send_sem=sems[0].at[k], recv_sem=sems[1].at[k],
        device_id=where, device_id_type=MESH,
    )


def whole_kernel(
    n, rows, norm, modes, group, owners, plan,
    x_hbm, g_hbm, res_hbm, log_hbm, waves_hbm, angle_hbm,
    y_ref, gs_ref, gathered_ref, grate_ref,
    x_ref, g_ref, res_ref, log_ref, waves_ref, angle_ref, decay_ref, rates_ref, rows_ref,
    state_ref, weighted_ref, x_hat_ref, g_hat_ref, sum_ref, moment_ref,
    pair_ref, total_ref, outer_ref, back_ref, landed_ref, sum_pair_ref, owned_ref,
    reduced_ref, rate_row_ref, rate_seq_ref,
    in_sems, *sems,
):
    length, channels = x_ref.shape
    groups = log_ref.shape[1]
    half = channels // 2
    chunk = SUB * LANES
    count = half // chunk
    steps = 2 * count
    outer = n // 2
    me = lax.axis_index("seq")
    mine = lax.axis_index("batch")
    z, side = lax.div(me, 2), lax.rem(me, 2)
    own_base, pair_base = side * half, (1 - side) * half
    unit = half // (rows * owners)
    pairs = [(sems[2 * i], sems[2 * i + 1]) for i in range(len(sems) // 2)]
    partner = {"seq": me + 1 - 2 * side}

    def lanes(start, width=chunk):
        return pl.ds(pl.multiple_of(start, TILE), width)

    def base_of(j):
        return jnp.where(j < count, pair_base + j * chunk, own_base + (j - count) * chunk)

    def loads(j):
        here = lanes(base_of(j))
        return [
            pltpu.make_async_copy(x_hbm.at[:, here], x_ref.at[:, here], in_sems.at[j]),
            pltpu.make_async_copy(g_hbm.at[:, here], g_ref.at[:, here], in_sems.at[steps + j]),
        ]

    load_log = pltpu.make_async_copy(log_hbm, log_ref, in_sems.at[2 * steps])
    late = [
        pltpu.make_async_copy(source, target, in_sems.at[2 * steps + 1 + i])
        for i, (source, target) in enumerate(
            ((waves_hbm, waves_ref), (angle_hbm, angle_ref), (res_hbm, res_ref))
        )
    ]

    def to_pair(k):
        here = lanes(pair_base + k * chunk)
        return remote(
            state_ref.at[:, :, here], pair_ref.at[:, :, lanes(k * chunk)], pairs[0], k, partner
        )

    def to_outer(k):
        out = []
        for i in range(1, outer):
            peer = lax.rem(z + i, outer)
            here = lanes(k * chunk)
            out.append(
                remote(
                    total_ref.at[jnp.where(peer > z, 0, 1), :, here], outer_ref.at[z, :, here],
                    pairs[1], (i - 1) * count + k, {"seq": 2 * peer + side},
                )
            )
        return out

    def to_back(k):
        return remote(
            back_ref.at[:, :, lanes(k * chunk)], landed_ref.at[:, :, lanes(own_base + k * chunk)],
            pairs[2], k, partner,
        )

    def sums_to_pair():
        return remote(sum_ref.at[:, lanes(pair_base, half)], sum_pair_ref, pairs[3], 0, partner)

    def owned_at(q, zo):
        return q * (half // rows) + zo * unit

    def guarded(condition, action):
        if owners == outer:
            action()
        else:
            pl.when(condition)(action)

    near = [(q, i) for q in range(rows) for i in range(outer) if q or i]
    far = [(q, i) for q in range(rows) for i in range(n) if q or i]

    def reduce_copy(k):
        q, i = near[k]
        peer_q, peer_z = lax.rem(mine + q, rows), lax.rem(z + i, outer)
        return peer_z, remote(
            owned_ref.at[:, lanes(owned_at(peer_q, jnp.minimum(peer_z, owners - 1)), unit)],
            reduced_ref.at[k], pairs[4], k, {"batch": peer_q, "seq": 2 * peer_z + side},
        )

    def gather_copy(k):
        q, i = far[k]
        here = lanes(own_base + owned_at(mine, jnp.minimum(z, owners - 1)), unit)
        return lax.div(lax.rem(me + n - i, n), 2), remote(
            gathered_ref.at[:, here], gathered_ref.at[:, here], pairs[5], k,
            {"batch": lax.rem(mine + q, rows), "seq": lax.rem(me + i, n)},
        )

    def rates_beside():
        return [
            remote(
                rate_row_ref.at[mine], rate_row_ref.at[mine], pairs[6], i - 1,
                {"batch": lax.rem(mine + i, rows)},
            )
            for i in range(1, rows)
        ]

    def rates_along():
        return [
            remote(
                rate_seq_ref.at[me], rate_seq_ref.at[me], pairs[7], i - 1,
                {"seq": lax.rem(me + i, n)},
            )
            for i in range(1, n)
        ]

    load_log.start()
    barrier = pltpu.get_barrier_semaphore()
    for copy in loads(0):
        copy.start()
    for q, i in far:
        pl.semaphore_signal(
            barrier, inc=1, device_id={"batch": lax.rem(mine + q, rows), "seq": lax.rem(me + i, n)},
            device_id_type=MESH,
        )
    for j in range(1, steps):
        for copy in loads(j):
            copy.start()
    for copy in late:
        copy.start()
    outer_ref[z] = jnp.zeros((modes, half), F32)

    load_log.wait()
    decay_ref[...] = jnp.exp(log_ref[...])
    lane = lax.broadcasted_iota(jnp.int32, (modes, TILE), 1)
    sub = lax.broadcasted_iota(jnp.int32, (modes, TILE), 0)
    per_tile = TILE // group
    for k in range(channels // TILE):
        first = k * per_tile
        tile = decay_ref[:, first // TILE * TILE : (first // TILE + 1) * TILE]
        rates_ref[:, k * TILE : (k + 1) * TILE] = pick_lanes(tile, lane // group + first % TILE)
    per_block = LANES // group
    for b in range(channels // LANES):
        first = b * per_block
        tile = decay_ref[:, first // TILE * TILE : (first // TILE + 1) * TILE]
        taken = pick_lanes(tile, lane // modes + first % TILE)
        row = jnp.sum(jnp.where(lane % modes == sub, taken, 0.0), axis=0, keepdims=True)
        rows_ref[b] = jnp.broadcast_to(row, (modes, TILE))

    def states(j, nothing):
        base = base_of(j)
        for copy in loads(j):
            copy.wait()
        for s in range(SUB):
            at = lanes(base + s * LANES, LANES)
            first = lax.div(base, group) + s * per_block
            tile = decay_ref[:, lanes(lax.div(first, TILE) * TILE, TILE)]
            shift = lax.rem(first, TILE)
            rate = jnp.concatenate(
                [pick_lanes(tile, jnp.full((modes, TILE), shift + g)) for g in range(per_block)], 0
            )
            (s_x, w_x), (s_g, w_g) = state_block(modes, group, rate, x_ref[:, at], g_ref[:, at])
            state_ref[0, :, at] = s_x
            state_ref[1, :, at] = s_g
            weighted_ref[0, :, at] = w_x
            weighted_ref[1, :, at] = w_g

        for k in range(count):
            @pl.when(j == k)
            def _():
                if k == 0:
                    pl.semaphore_wait(barrier, len(far))
                to_pair(k).start()

        return nothing

    lax.fori_loop(0, steps, states, 0)

    def both_of(k):
        at, here = lanes(own_base + k * chunk), lanes(k * chunk)
        first = side == 0
        ours, theirs = [state_ref[i, :, at] for i in (0, 1)], [pair_ref[i, :, here] for i in (0, 1)]
        a = [jnp.where(first, o, t) for o, t in zip(ours, theirs)]
        b = [jnp.where(first, t, o) for o, t in zip(ours, theirs)]
        return a, b, jnp.exp(-rates_ref[:, at] * float(length)), first, at, here

    def send_total(k):
        to_pair(k).wait_recv()
        a, b, whole, first, at, here = both_of(k)
        total_ref[0, :, here] = whole * a[0] + b[0]
        total_ref[1, :, here] = a[1] + whole * b[1]
        for copy in to_outer(k):
            copy.start()

    def take_total(k):
        for copy in to_outer(k):
            copy.wait_recv()
        a, b, whole, first, at, here = both_of(k)
        twofold = whole * whole
        carry = jnp.zeros_like(whole)
        adjoint = jnp.zeros_like(whole)
        for i in range(outer):
            carry = jnp.where(i < z, outer_ref[i, :, here] + twofold * carry, carry)
            last = outer - 1 - i
            adjoint = jnp.where(last > z, outer_ref[last, :, here] + twofold * adjoint, adjoint)
        carry_b = whole * carry + a[0]
        adjoint_a = whole * adjoint + b[1]
        back_ref[0, :, here] = jnp.where(first, carry_b, carry)
        back_ref[1, :, here] = jnp.where(first, adjoint, adjoint_a)
        to_back(k).start()
        landed_ref[0, :, at] = jnp.where(first, carry, carry_b)
        landed_ref[1, :, at] = jnp.where(first, adjoint_a, adjoint)
        fold = 1.0 / (1.0 + whole)
        cross = (carry + a[0] * fold) * a[1] + (carry_b + b[0] * fold) * b[1]
        owned_ref[:, here] = jnp.exp(-rates_ref[:, at]) * cross

    def start_reduce():
        sums_to_pair().wait_recv()
        owned_ref[...] = owned_ref[...] + (sum_ref[:, lanes(own_base, half)] + sum_pair_ref[...])
        for k in range(len(near)):
            peer_z, copy = reduce_copy(k)
            guarded(peer_z < owners, copy.start)

    def start_rates():
        many = TILE // per_block
        row_id = lax.broadcasted_iota(jnp.int32, (LANES, TILE), 0) // group
        col_id = lax.broadcasted_iota(jnp.int32, (LANES, TILE), 1)

        def lap(c, nothing):
            added = jnp.zeros((2 * modes, TILE), F32)
            for j in range(many):
                at = lanes((c * many + j) * LANES, LANES)
                rate = rates_ref[:, at]
                pole = jnp.exp(-rate)
                whole = jnp.exp(-rate * float(length))
                fold = 1.0 / (1.0 + whole)
                turned_x, turned_g = state_ref[0, :, at] * fold, state_ref[1, :, at] * fold
                carry, adjoint = landed_ref[0, :, at], landed_ref[1, :, at]
                carry_all, adjoint_all = carry + turned_x, adjoint + turned_g
                moments = (
                    moment_ref[:, at]
                    + pole * (carry_all * weighted_ref[1, :, at] + adjoint_all * weighted_ref[0, :, at])
                    + float(length) * pole * whole * (carry * adjoint - turned_x * turned_g)
                )
                pick = jnp.where(row_id + j * per_block == col_id, 1.0, 0.0).astype(BF16)
                added += mul(jnp.concatenate(split(-rate * res_ref[:, at] * moments), 0), pick)
            rate_row_ref[mine, :, lanes(c * TILE, TILE)] = added[:modes] + added[modes:]
            return nothing

        lax.fori_loop(0, groups // TILE, lap, 0)
        for copy in rates_beside():
            copy.start()

    for copy in late:
        copy.wait()

    def lags(j, nothing):
        for k in range(count):
            @pl.when(j == plan["total"][k])
            def _():
                send_total(k)

        base = base_of(j)
        for s in range(SUB):
            at = lanes(base + s * LANES, LANES)
            rate = rows_ref[lax.div(base, LANES) + s, 0:1, :]
            x_hat, g_hat, sums, moments = lag_block(
                modes, group, rate, waves_ref[0], angle_ref[...], x_ref[:, at], g_ref[:, at]
            )
            x_hat_ref[:, at] = x_hat
            g_hat_ref[:, at] = g_hat
            sum_ref[:, at] = sums
            moment_ref[:, at] = moments

        @pl.when(j == count - 1)
        def _():
            sums_to_pair().start()

        for k in range(count):
            if plan["take"][k] < steps:
                @pl.when(j == plan["take"][k])
                def _():
                    take_total(k)

        return nothing

    lax.fori_loop(0, steps, lags, 0)

    order = plan["order"]

    def base_out(j):
        base = own_base
        for i, (own, k) in enumerate(order):
            base = jnp.where(j == i, (own_base if own else pair_base) + k * chunk, base)
        return base

    def outs(j, nothing):
        for k in range(count):
            if plan["take"][k] >= steps:
                @pl.when(j == plan["take"][k] - steps)
                def _():
                    take_total(k)

        for i, (own, k) in enumerate(order):
            if not own:
                @pl.when(j == i)
                def _():
                    to_back(k).wait_recv()

        @pl.when(j == plan["reduce"])
        def _():
            start_reduce()

        @pl.when(j == plan["rates"])
        def _():
            start_rates()

        base = base_out(j)
        for s in range(SUB):
            at = lanes(base + s * LANES, LANES)
            rate = rows_ref[lax.div(base, LANES) + s, 0:1, :]
            res = res_ref[:, at]
            fold = 1.0 / (1.0 + jnp.exp(-rates_ref[:, at] * float(length)))
            start_x = res * (landed_ref[0, :, at] + state_ref[0, :, at] * fold)
            start_g = res * (landed_ref[1, :, at] + state_ref[1, :, at] * fold)
            y, gs = out_block(
                group, rate, waves_ref[1, :, :length], waves_ref[1, :, length:], angle_ref[...],
                x_hat_ref[:, at], g_hat_ref[:, at], res, start_x, start_g,
            )
            y_ref[:, at] = y.astype(BF16)
            gs_ref[:, at] = gs.astype(BF16)
        return nothing

    lax.fori_loop(0, steps, outs, 0)

    def finish_reduce():
        part = owned_ref[:, lanes(owned_at(mine, jnp.minimum(z, owners - 1)), unit)]
        for k in range(len(near)):
            reduce_copy(k)[1].wait_recv()
            part = part + reduced_ref[k]
        gathered_ref[:, lanes(own_base + owned_at(mine, jnp.minimum(z, owners - 1)), unit)] = part * norm
        for k in range(len(far)):
            gather_copy(k)[1].start()

    guarded(z < owners, finish_reduce)
    for copy in rates_beside():
        copy.wait_recv()
    part = rate_row_ref[0]
    for i in range(1, rows):
        part = part + rate_row_ref[i]
    rate_seq_ref[me] = part
    for copy in rates_along():
        copy.start()
    for copy in rates_along():
        copy.wait_recv()
    part = rate_seq_ref[0]
    for i in range(1, n):
        part = part + rate_seq_ref[i]
    grate_ref[...] = part * norm
    for k in range(len(far)):
        from_z, copy = gather_copy(k)
        guarded(from_z < owners, copy.wait_recv)

    for k in range(count):
        for copy in [to_pair(k), to_back(k)] + to_outer(k):
            copy.wait_send()
    sums_to_pair().wait_send()
    for k in range(len(near)):
        peer_z, copy = reduce_copy(k)
        guarded(peer_z < owners, copy.wait_send)
    for k in range(len(far)):
        guarded(z < owners, gather_copy(k)[1].wait_send)
    for copy in rates_beside() + rates_along():
        copy.wait_send()


def constants(length):
    half = length // 2
    omega = np.pi * (2.0 * np.arange(half) + 1.0) / length
    at = np.arange(length)
    forward = np.concatenate([np.cos(np.outer(omega, at)), -np.sin(np.outer(omega, at))], axis=0)
    lanes = np.ones((1, TILE))
    angle = np.stack(
        [2.0 * np.sin(omega / 2.0)[:, None] ** 2 * lanes, np.sin(omega)[:, None] * lanes]
    )
    return forward.astype(np.float32), (forward.T / half).astype(np.float32), angle.astype(np.float32)


def plan_of(count):
    own = [(True, k) for k in range(count)]
    pair = [(False, k) for k in range(count)]
    order = own[:2] + [v for both in zip(pair, own[2:] + [None] * 2) for v in both if v]
    return {
        "total": [min(2 * count - 1, k + 1) for k in range(count)],
        "take": [2 * count + order.index((True, k)) for k in range(count)],
        "order": order,
        "reduce": min(2 * count - 1, order.index((True, count - 1)) + 1),
        "rates": 2 * count - 1,
    }


def leave_kernel(*refs):
    count = len(refs) // 2
    sems = refs[-1]
    copies = []
    for i, (source, target) in enumerate(zip(refs[:count], refs[count:])):
        copies.append(pltpu.make_async_copy(source, target, sems.at[i]))
    for copy in copies:
        copy.start()
    for copy in copies:
        copy.wait()


def leave(*arrays):
    return pl.pallas_call(
        leave_kernel,
        in_specs=[pl.BlockSpec(memory_space=pltpu.VMEM)] * len(arrays),
        out_specs=[pl.BlockSpec(memory_space=pltpu.HBM)] * len(arrays),
        out_shape=[pltpu.HBM(a.shape, a.dtype) for a in arrays],
        scratch_shapes=[pltpu.SemaphoreType.DMA((len(arrays),))],
        compiler_params=pltpu.CompilerParams(vmem_limit_bytes=4 * 1024 * 1024),
    )(*[pltpu.with_memory_space_constraint(a, pltpu.VMEM) for a in arrays])


def local(mesh_shape, signal, out_grad, residues, log_rates):
    batch_rows, length, channels = signal.shape
    modes, groups = log_rates.shape
    group = channels // groups
    n, rows = mesh_shape["seq"], mesh_shape["batch"]
    norm = 1.0 / (batch_rows * rows * length * n)
    forward, inverse, angle = constants(length)
    dft = np.asarray(forward).astype(jnp.bfloat16)
    dft = np.concatenate([dft, (forward - dft.astype(np.float32)).astype(jnp.bfloat16)], axis=1)
    inv_high = np.asarray(inverse).astype(jnp.bfloat16)
    inv_low = (inverse - inv_high.astype(np.float32)).astype(jnp.bfloat16)
    waves = np.stack([dft, np.concatenate([inv_high, inv_low], axis=1)])
    half = channels // 2
    outer = n // 2
    count = half // (SUB * LANES)
    steps = 2 * count
    owners = min(outer, half // (rows * TILE))
    unit = half // (rows * owners)

    def dma(size):
        return pltpu.SemaphoreType.DMA((max(size, 1),))

    def vmem(*shape, dtype=F32):
        return pltpu.VMEM(shape, dtype)

    hbm_spec = pl.BlockSpec(memory_space=pltpu.HBM)
    vmem_spec = pl.BlockSpec(memory_space=pltpu.VMEM)
    links = [count, (outer - 1) * count, count, 1, rows * outer - 1, rows * n - 1, rows - 1, n - 1]
    mixed, grads, res_sum, rate_sum = [], [], 0.0, 0.0
    for row in range(batch_rows):
        held = (
            signal[row], out_grad[row], residues, log_rates, jnp.asarray(waves), jnp.asarray(angle)
        )
        y, gs, part, rates = pl.pallas_call(
            functools.partial(whole_kernel, n, rows, norm, modes, group, owners, plan_of(count)),
            in_specs=[hbm_spec] * 6,
            out_specs=[vmem_spec] * 4,
            out_shape=[
                vmem(length, channels, dtype=BF16),
                vmem(length, channels, dtype=BF16),
                vmem(modes, channels),
                vmem(modes, groups),
            ],
            scratch_shapes=[
                vmem(length, channels, dtype=BF16),
                vmem(length, channels, dtype=BF16),
                vmem(modes, channels),
                vmem(modes, groups),
                vmem(*waves.shape, dtype=BF16),
                vmem(*angle.shape),
                vmem(modes, groups),
                vmem(modes, channels),
                vmem(channels // LANES, modes, TILE),
                vmem(2, modes, channels),
                vmem(2, modes, channels),
                vmem(length, channels),
                vmem(length, channels),
                vmem(modes, channels),
                vmem(modes, channels),
                vmem(2, modes, half),
                vmem(2, modes, half),
                vmem(outer, modes, half),
                vmem(2, modes, half),
                vmem(2, modes, channels),
                vmem(modes, half),
                vmem(modes, half),
                vmem(max(rows * outer - 1, 1), modes, unit),
                vmem(rows, modes, groups),
                vmem(n, modes, groups),
                dma(2 * steps + 4),
            ]
            + [dma(size) for size in links for _ in range(2)],
            compiler_params=pltpu.CompilerParams(
                collective_id=0, has_side_effects=True, vmem_limit_bytes=32 * 1024 * 1024
            ),
        )(*[pltpu.with_memory_space_constraint(a, pltpu.HBM) for a in held])
        y, gs, part, rates = leave(y, gs, part, rates)
        mixed.append(y)
        grads.append(gs)
        res_sum = res_sum + part if row else part
        rate_sum = rate_sum + rates if row else rates
    return jnp.stack(mixed), jnp.stack(grads), res_sum, rate_sum


def solution(mesh):
    placed = (P("batch", "seq", None), P("batch", "seq", None), P(), P())
    return jax.shard_map(
        functools.partial(local, dict(mesh.shape)),
        mesh=mesh,
        in_specs=placed,
        out_specs=placed,
        check_vma=False,
    )
```

```python
import functools

import jax
import jax.numpy as jnp
import numpy as np
from jax import lax
from jax.experimental import pallas as pl
from jax.experimental.pallas import tpu as pltpu
from jax.sharding import PartitionSpec as P

LANES = 256
TILE = 128
SUB = 4
F32 = jnp.float32
BF16 = jnp.bfloat16
MESH = pl.DeviceIdType.MESH


def split(value):
    high = value.astype(BF16)
    return high, (value - high.astype(F32)).astype(BF16)


def mul(a, b):
    return jnp.dot(a, b, preferred_element_type=F32)


def twice(value, axis):
    return jnp.concatenate([value, value], axis=axis)


def own_rows(wide, modes, group):
    rows, lanes = wide.shape
    owner = lax.broadcasted_iota(jnp.int32, (modes, lanes), 1) // group
    out = wide[:modes]
    for g in range(1, rows // modes):
        out = jnp.where(owner == g, wide[g * modes : (g + 1) * modes], out)
    return out


def pick_lanes(tile, index):
    return jnp.take_along_axis(tile, index, axis=1, mode="promise_in_bounds")


def state_block(modes, group, rate, x, g):
    rows, length = rate.shape
    lane = lax.broadcasted_iota(jnp.int32, (rows, length), 1)
    at = lane.astype(F32)
    rising = jnp.exp(-rate * at)
    falling = pick_lanes(rising, length - 1 - lane)
    out = []
    for table, weight, values in ((falling, length - at, x), (rising, at, g)):
        left = jnp.concatenate([table, weight * table], axis=0)
        both = mul(jnp.concatenate(split(left), axis=1), twice(values, 0))
        out.append((own_rows(both[:rows], modes, group), own_rows(both[rows:], modes, group)))
    return out


def phi_of(pole, gap, angle):
    near = pole * angle[0]
    inverse = 1.0 / (gap * gap + (near + near))
    return (gap + near) * inverse, pole * angle[1] * inverse


def full(high, low):
    return jnp.concatenate([twice(high, 1), twice(low, 1)], axis=0)


def fold_rows(value):
    rows = value.shape[0] // 2
    return value[:rows] + value[rows:]


def lag_block(modes, group, pole, gap, angle, x_hat, g_hat):
    half = x_hat.shape[0] // 2
    r, i = phi_of(pole, gap, angle)
    lower = lax.broadcasted_iota(jnp.int32, r.shape, 1) < half
    terms = []
    for a, b in ((r, i), (r * r - i * i - r, 2.0 * r * i - i)):
        terms += [jnp.where(lower, a, pltpu.roll(b, half, 1)), jnp.where(lower, pltpu.roll(a, half, 1), b)]
    gm = 2 * r.shape[0]
    xr, xi = x_hat[:half], x_hat[half:]
    gr, gi = g_hat[:half], g_hat[half:]
    lag = jnp.concatenate([gr * xr + gi * xi, gr * xi - gi * xr], axis=0) * (1.0 / half)
    left = full(*split(jnp.concatenate(terms, axis=0)))
    wide = fold_rows(mul(left, jnp.concatenate(split(lag), axis=0)))
    return own_rows(wide[:gm], modes, group), own_rows(wide[gm:], modes, group)


def spread(narrow, mask):
    high, low = split(twice(narrow, 0))
    times = mask.shape[0] // high.shape[0]
    return jnp.concatenate(
        [jnp.concatenate([part] * times, axis=0) * mask for part in (high, low)], axis=0
    )


def hat_block(rate, mask, angle, x_hat, g_hat, res, start_x, start_g):
    half = x_hat.shape[0] // 2
    pole = jnp.exp(-rate)
    left = full(*split(jnp.concatenate(phi_of(pole, gap_of(rate), angle), axis=0)))
    right = jnp.concatenate([spread(v, mask) for v in (res, start_x, start_g)], axis=1)
    wide = fold_rows(mul(left, right))
    lanes = res.shape[1]
    (kr, ki), (cr, ci), (ar, ai) = [
        (wide[:half, at : at + lanes], wide[half:, at : at + lanes]) for at in (0, lanes, 2 * lanes)
    ]
    xr, xi = x_hat[:half], x_hat[half:]
    gr, gi = g_hat[:half], g_hat[half:]
    level = jnp.sum(start_g, axis=0, keepdims=True)
    y_hat = jnp.concatenate([kr * xr + ki * xi + cr, kr * xi - ki * xr - ci], axis=0)
    h_hat = jnp.concatenate([kr * gr - ki * gi + (level - ar), kr * gi + ki * gr - ai], axis=0)
    return jnp.concatenate(split(y_hat), axis=0), jnp.concatenate(split(h_hat), axis=0)


def gap_of(rate):
    gap = jnp.ones_like(rate)
    for k in range(7, 1, -1):
        gap = 1.0 - rate * gap * (1.0 / k)
    return rate * gap


def remote(source, target, sems, k, where):
    return pltpu.make_async_remote_copy(
        src_ref=source, dst_ref=target, send_sem=sems[0].at[k], recv_sem=sems[1].at[k],
        device_id=where, device_id_type=MESH,
    )


def whole_kernel(
    n, rows, norm, modes, group, owners, plan,
    x_hbm, g_hbm, res_hbm, log_hbm, waves_hbm, angle_hbm,
    y_ref, gs_ref, gathered_ref, grate_ref,
    x_ref, g_ref, res_ref, log_ref, waves_ref, angle_ref, decay_ref, pole_ref, gap_ref, rates_ref, rows_ref,
    state_ref, weighted_ref, x_hat_ref, g_hat_ref, hat_ref, sum_ref, moment_ref, cross_ref,
    pair_ref, weighted_pair_ref, total_ref, outer_ref, back_ref, landed_ref, sum_pair_ref, owned_ref,
    reduced_ref, rate_row_ref, rate_seq_ref,
    in_sems, *sems,
):
    length, channels = x_ref.shape
    groups = log_ref.shape[1]
    half = channels // 2
    chunk = SUB * LANES
    count = half // chunk
    steps = 2 * count
    outer = n // 2
    me = lax.axis_index("seq")
    mine = lax.axis_index("batch")
    z, side = lax.div(me, 2), lax.rem(me, 2)
    own_base, pair_base = side * half, (1 - side) * half
    unit = half // (rows * owners)
    pairs = [(sems[2 * i], sems[2 * i + 1]) for i in range(len(sems) // 2)]
    partner = {"seq": me + 1 - 2 * side}

    def lanes(start, width=chunk):
        return pl.ds(pl.multiple_of(start, TILE), width)

    def base_of(j):
        return jnp.where(j < count, pair_base + j * chunk, own_base + (j - count) * chunk)

    def loads(j):
        here = lanes(base_of(j))
        return [
            pltpu.make_async_copy(x_hbm.at[:, here], x_ref.at[:, here], in_sems.at[j]),
            pltpu.make_async_copy(g_hbm.at[:, here], g_ref.at[:, here], in_sems.at[steps + j]),
        ]

    load_log = pltpu.make_async_copy(log_hbm, log_ref, in_sems.at[2 * steps])
    late = [
        pltpu.make_async_copy(source, target, in_sems.at[2 * steps + 1 + i])
        for i, (source, target) in enumerate(
            ((waves_hbm, waves_ref), (angle_hbm, angle_ref), (res_hbm, res_ref))
        )
    ]

    def to_pair(k):
        here = lanes(pair_base + k * chunk)
        return remote(
            state_ref.at[:, :, here], pair_ref.at[:, :, lanes(k * chunk)], pairs[0], k, partner
        )

    def weights_to_pair():
        return remote(
            weighted_ref.at[:, :, lanes(pair_base, half)], weighted_pair_ref, pairs[9], 0, partner
        )

    def to_outer(k):
        out = []
        for i in range(1, outer):
            peer = lax.rem(z + i, outer)
            here = lanes(k * chunk)
            out.append(
                remote(
                    total_ref.at[jnp.where(peer > z, 0, 1), :, here], outer_ref.at[z, :, here],
                    pairs[1], (i - 1) * count + k, {"seq": 2 * peer + side},
                )
            )
        return out

    def to_back(k):
        return remote(
            back_ref.at[:, :, lanes(k * chunk)], landed_ref.at[:, :, lanes(own_base + k * chunk)],
            pairs[2], k, partner,
        )

    def sums_to_pair():
        return remote(sum_ref.at[:, lanes(pair_base, half)], sum_pair_ref, pairs[3], 0, partner)

    def owned_at(q, zo):
        return q * (half // rows) + zo * unit

    def guarded(condition, action):
        if owners == outer:
            action()
        else:
            pl.when(condition)(action)

    near = [(q, i) for q in range(rows) for i in range(outer) if q or i]
    stride = 2 if rows % 2 == 0 else 1
    far = [(q, i) for q in range(0, rows, stride) for i in range(n) if q or i]
    known = [(q, i) for q in range(rows) for i in range(n) if (q or i) and (q % stride == 0 or i % 2 == 0)]

    def reduce_copy(k):
        q, i = near[k]
        peer_q, peer_z = lax.rem(mine + q, rows), lax.rem(z + i, outer)
        return peer_z, remote(
            owned_ref.at[:, lanes(owned_at(peer_q, jnp.minimum(peer_z, owners - 1)), unit)],
            reduced_ref.at[k], pairs[4], k, {"batch": peer_q, "seq": 2 * peer_z + side},
        )

    def gather_copy(k):
        q, i = far[k]
        here = lanes(own_base + owned_at(mine, jnp.minimum(z, owners - 1)), unit)
        return lax.div(lax.rem(me + n - i, n), 2), remote(
            gathered_ref.at[:, here], gathered_ref.at[:, here], pairs[5], k,
            {"batch": lax.rem(mine + q, rows), "seq": lax.rem(me + i, n)},
        )

    def spread_copies():
        if stride == 1:
            return []
        odd = lax.rem(mine, 2)
        width = half // rows
        out = []
        for i in range(2):
            for t in range(rows // 2):
                here = lanes(i * half + (odd + 2 * t) * width, width)
                out.append(
                    remote(
                        gathered_ref.at[:, here], gathered_ref.at[:, here], pairs[8],
                        i * (rows // 2) + t, {"batch": mine + 1 - 2 * odd},
                    )
                )
        return out

    def rates_beside():
        return [
            remote(
                rate_row_ref.at[mine], rate_row_ref.at[mine], pairs[6], i - 1,
                {"batch": lax.rem(mine + i, rows)},
            )
            for i in range(1, rows)
        ]

    def rates_along():
        return [
            remote(
                rate_seq_ref.at[me], rate_seq_ref.at[me], pairs[7], i - 1,
                {"seq": lax.rem(me + i, n)},
            )
            for i in range(1, n)
        ]

    load_log.start()
    barrier = pltpu.get_barrier_semaphore()
    for copy in loads(0):
        copy.start()
    for q, i in known:
        pl.semaphore_signal(
            barrier, inc=1, device_id={"batch": lax.rem(mine + q, rows), "seq": lax.rem(me + i, n)},
            device_id_type=MESH,
        )
    for j in range(1, steps):
        for copy in loads(j):
            copy.start()
    for copy in late:
        copy.start()
    outer_ref[z] = jnp.zeros((modes, half), F32)

    load_log.wait()
    decay = jnp.exp(log_ref[...])
    decay_ref[...] = decay
    pole_ref[...] = jnp.exp(-decay)
    gap_ref[...] = gap_of(decay)
    per_block = LANES // group

    def tile_of(base, s):
        first = lax.div(base, group) + s * per_block
        return lanes(lax.div(first, TILE) * TILE, TILE), lax.rem(first, TILE)

    def states(j, nothing):
        base = base_of(j)
        for copy in loads(j):
            copy.wait()
        for s in range(SUB):
            at = lanes(base + s * LANES, LANES)
            tile, shift = tile_of(base, s)
            rate = jnp.concatenate(
                [
                    pick_lanes(decay_ref[:, tile], jnp.full((modes, TILE), shift + g))
                    for g in range(per_block)
                ],
                0,
            )
            (s_x, w_x), (s_g, w_g) = state_block(modes, group, rate, x_ref[:, at], g_ref[:, at])
            state_ref[0, :, at] = s_x
            state_ref[1, :, at] = s_g
            weighted_ref[0, :, at] = w_x
            weighted_ref[1, :, at] = w_g

        for k in range(count):
            @pl.when(j == k)
            def _():
                if k == 0:
                    pl.semaphore_wait(barrier, len(known))
                to_pair(k).start()

        return nothing

    lax.fori_loop(0, steps, states, 0)

    lane = lax.broadcasted_iota(jnp.int32, (modes, TILE), 1)
    sub = lax.broadcasted_iota(jnp.int32, (modes, TILE), 0)
    per_tile = TILE // group
    for k in range(channels // TILE):
        first = k * per_tile
        tile = decay_ref[:, first // TILE * TILE : (first // TILE + 1) * TILE]
        rates_ref[:, k * TILE : (k + 1) * TILE] = pick_lanes(tile, lane // group + first % TILE)
    for b in range(channels // LANES):
        first = b * per_block
        tile = decay_ref[:, first // TILE * TILE : (first // TILE + 1) * TILE]
        taken = pick_lanes(tile, lane // modes + first % TILE)
        row = jnp.sum(jnp.where(lane % modes == sub, taken, 0.0), axis=0, keepdims=True)
        rows_ref[b] = jnp.broadcast_to(row, (modes, TILE))

    def both_of(k):
        at, here = lanes(own_base + k * chunk), lanes(k * chunk)
        first = side == 0
        ours, theirs = [state_ref[i, :, at] for i in (0, 1)], [pair_ref[i, :, here] for i in (0, 1)]
        a = [jnp.where(first, o, t) for o, t in zip(ours, theirs)]
        b = [jnp.where(first, t, o) for o, t in zip(ours, theirs)]
        return a, b, jnp.exp(-rates_ref[:, at] * float(length)), first, at, here

    def send_total(k):
        to_pair(k).wait_recv()
        a, b, whole, first, at, here = both_of(k)
        total_ref[0, :, here] = whole * a[0] + b[0]
        total_ref[1, :, here] = a[1] + whole * b[1]
        for copy in to_outer(k):
            copy.start()

    def take_total(k):
        for copy in to_outer(k):
            copy.wait_recv()
        a, b, whole, first, at, here = both_of(k)
        twofold = whole * whole
        carry = jnp.zeros_like(whole)
        adjoint = jnp.zeros_like(whole)
        for i in range(outer):
            carry = jnp.where(i < z, outer_ref[i, :, here] + twofold * carry, carry)
            last = outer - 1 - i
            adjoint = jnp.where(last > z, outer_ref[last, :, here] + twofold * adjoint, adjoint)
        carry_b = whole * carry + a[0]
        adjoint_a = whole * adjoint + b[1]
        back_ref[0, :, here] = jnp.where(first, carry_b, carry)
        back_ref[1, :, here] = jnp.where(first, adjoint, adjoint_a)
        to_back(k).start()
        landed_ref[0, :, at] = jnp.where(first, carry, carry_b)
        landed_ref[1, :, at] = jnp.where(first, adjoint_a, adjoint)
        if k == 0:
            weights_to_pair().wait_recv()
        ours = [weighted_ref[i, :, at] for i in (0, 1)]
        theirs = [weighted_pair_ref[i, :, here] for i in (0, 1)]
        cross, moments = jnp.zeros_like(whole), jnp.zeros_like(whole)
        for (s_x, s_g), (w_x, w_g), into, back in (
            (a, [jnp.where(first, o, t) for o, t in zip(ours, theirs)], carry, adjoint_a),
            (b, [jnp.where(first, t, o) for o, t in zip(ours, theirs)], carry_b, adjoint),
        ):
            turned_x, turned_g = s_x / (1.0 + whole), s_g / (1.0 + whole)
            into_all = into + turned_x
            cross += into_all * s_g
            moments += (into_all * w_g + (back + turned_g) * w_x) + float(length) * whole * (
                into * back - turned_x * turned_g
            )
        rate = rates_ref[:, at]
        pole = jnp.exp(-rate)
        owned_ref[:, here] = pole * cross
        cross_ref[:, here] = -rate * res_ref[:, at] * pole * moments

    def group_sums(value):
        parts = [value[:, t * TILE : (t + 1) * TILE] for t in range(value.shape[1] // TILE)]
        many, shift = len(parts), 1
        while shift < group:
            if len(parts) > 1:
                low = (lane & shift) == 0
                parts = [
                    jnp.where(low, a, b) + pick_lanes(jnp.where(low, b, a), lane ^ shift)
                    for a, b in zip(parts[::2], parts[1::2])
                ]
            else:
                parts = [parts[0] + pick_lanes(parts[0], lane ^ shift)]
            shift *= 2
        return pick_lanes(parts[0], lane % per_tile * group + lane // per_tile % many)

    def start_reduce(nothing):
        sums_to_pair().wait_recv()
        owned_ref[...] = owned_ref[...] + (sum_ref[:, lanes(own_base, half)] + sum_pair_ref[...])
        for k in range(len(near)):
            peer_z, copy = reduce_copy(k)
            guarded(peer_z < owners, copy.start)

    def start_rates(nothing):
        own = lanes(own_base, half)
        moment_ref[:, own] = moment_ref[:, own] + cross_ref[...]
        held = TILE * group // chunk
        for t in range(groups // TILE):
            out = jnp.zeros((modes, TILE), F32)
            for i in range(held):
                base = (t * held + i) * chunk
                sums = group_sums(moment_ref[:, base : base + chunk])
                out = jnp.where(lane // (TILE // held) == i, sums, out)
            rate_row_ref[mine, :, t * TILE : (t + 1) * TILE] = out
        for copy in rates_beside():
            copy.start()

    def start_gather(nothing):
        own_at = owned_at(mine, jnp.minimum(z, owners - 1))

        def finish_reduce():
            part = owned_ref[:, lanes(own_at, unit)]
            for k in range(len(near)):
                reduce_copy(k)[1].wait_recv()
                part = part + reduced_ref[k]
            gathered_ref[:, lanes(own_base + own_at, unit)] = part * norm
            for k in range(len(far)):
                gather_copy(k)[1].start()

        guarded(z < owners, finish_reduce)

    def start_along(nothing):
        for copy in rates_beside():
            copy.wait_recv()
        part = rate_row_ref[0]
        for i in range(1, rows):
            part = part + rate_row_ref[i]
        rate_seq_ref[me] = part
        for copy in rates_along():
            copy.start()

    events = {
        "total": send_total, "take": take_total, "reduce": start_reduce, "gather": start_gather,
        "rates": start_rates, "along": start_along,
        "back": lambda k: to_back(k).wait_recv(), "sums": lambda k: sums_to_pair().start(),
    }

    def run_events(phase, j):
        for step, name, k in plan[phase]:
            @pl.when(j == step)
            def _():
                events[name](k)

    def lags(j, nothing):
        run_events("lags", j)
        base = base_of(j)
        here = lanes(base)
        x_hat_ref[:, here] = mul(waves_ref[0], twice(x_ref[:, here], 0))
        g_hat_ref[:, here] = mul(waves_ref[0], twice(g_ref[:, here], 0))
        for s in range(SUB):
            at = lanes(base + s * LANES, LANES)
            tile, shift = tile_of(base, s)
            upper = jnp.where(lane < length // 2, shift, shift + per_block // 2)
            pole, gap = [
                jnp.concatenate(
                    [pick_lanes(ref[:, tile], upper + g) for g in range(per_block // 2)], 0
                )
                for ref in (pole_ref, gap_ref)
            ]
            sums, moments = lag_block(
                modes, group, pole, gap, angle_ref[:, length // 2 :][:, :1],
                x_hat_ref[:, at], g_hat_ref[:, at],
            )
            sum_ref[:, at] = sums
            moment_ref[:, at] = -rates_ref[:, at] * res_ref[:, at] * moments
        return nothing

    for copy in late:
        copy.wait()
    weights_to_pair().start()
    send_total(0)
    lax.fori_loop(0, steps, lags, 0)

    order = plan["order"]

    def base_out(j):
        base = own_base
        for i, (own, k) in enumerate(order):
            base = jnp.where(j == i, (own_base if own else pair_base) + k * chunk, base)
        return base

    def outs(j, nothing):
        run_events("outs", j)
        base = base_out(j)
        for s in range(SUB):
            at = lanes(base + s * LANES, LANES)
            rate = rows_ref[lax.div(base, LANES) + s, 0:1, :]
            res = res_ref[:, at]
            pole = jnp.exp(-rates_ref[:, at])
            above = 1.0 + jnp.exp(-rates_ref[:, at] * float(length))
            start_x = res * pole * (above * landed_ref[0, :, at] + state_ref[0, :, at])
            start_g = res * (above * landed_ref[1, :, at] + state_ref[1, :, at])
            y_hat, h_hat = hat_block(
                rate, waves_ref[3], angle_ref[:, : length // 2],
                x_hat_ref[:, at], g_hat_ref[:, at], res, start_x, start_g,
            )
            hat_ref[0, :, s * LANES : (s + 1) * LANES] = y_hat
            hat_ref[1, :, s * LANES : (s + 1) * LANES] = h_hat
        inverse = jnp.concatenate([waves_ref[1], waves_ref[2]], axis=0)
        here = lanes(base)
        y_ref[:, here] = fold_rows(mul(inverse, hat_ref[0])).astype(BF16)
        gs_ref[:, here] = fold_rows(mul(inverse, hat_ref[1])).astype(BF16)
        return nothing

    lax.fori_loop(0, steps, outs, 0)

    for k in range(len(far)):
        from_z, copy = gather_copy(k)
        guarded(from_z < owners, copy.wait_recv)
    for copy in spread_copies():
        copy.start()
    for copy in rates_along():
        copy.wait_recv()
    part = rate_seq_ref[0]
    for i in range(1, n):
        part = part + rate_seq_ref[i]
    grate_ref[...] = part * norm
    for copy in spread_copies():
        copy.wait_recv()

    for k in range(count):
        for copy in [to_pair(k), to_back(k)] + to_outer(k):
            copy.wait_send()
    sums_to_pair().wait_send()
    weights_to_pair().wait_send()
    for k in range(len(near)):
        peer_z, copy = reduce_copy(k)
        guarded(peer_z < owners, copy.wait_send)
    for k in range(len(far)):
        guarded(z < owners, gather_copy(k)[1].wait_send)
    for copy in rates_beside() + rates_along() + spread_copies():
        copy.wait_send()


def constants(length):
    half = length // 2
    omega = np.pi * (2.0 * np.arange(half) + 1.0) / length
    at = np.arange(length)
    forward = np.concatenate([np.cos(np.outer(omega, at)), -np.sin(np.outer(omega, at))], axis=0)
    parts = np.stack([2.0 * np.sin(omega / 2.0) ** 2, np.sin(omega)])
    angle = np.concatenate(
        [
            np.broadcast_to(parts[:, :, None], (2, half, 2 * half)),
            np.broadcast_to(np.tile(parts, (1, 2))[:, None], (2, 8, 2 * half)),
        ],
        axis=1,
    )
    return forward.astype(np.float32), (forward.T / half).astype(np.float32), angle.astype(np.float32)


def plan_of(count):
    last = 2 * count - 1
    own = [(True, k) for k in range(count)]
    pair = [(False, k) for k in range(count)]
    order = own[:2] + [v for both in zip(pair, own[2:] + [None] * 2) for v in both if v]
    lags = [(max(k - 1, 0), "total", k) for k in range(1, count)] + [(count, "sums", 0)]
    lags += [(7, "take", 0)]
    outs = [(t, "take", k + 1) for k, t in enumerate([0, 1, 1])]
    outs += [(1, "reduce", 0), (1, "rates", 0), (4, "gather", 0), (5, "along", 0)]
    outs += [(order.index(v), "back", v[1]) for v in pair]
    return {"lags": lags, "outs": outs, "order": order}


def leave_kernel(*refs):
    count = len(refs) // 2
    sems = refs[-1]
    copies = []
    for i, (source, target) in enumerate(zip(refs[:count], refs[count:])):
        copies.append(pltpu.make_async_copy(source, target, sems.at[i]))
    for copy in copies:
        copy.start()
    for copy in copies:
        copy.wait()


def leave(*arrays):
    return pl.pallas_call(
        leave_kernel,
        in_specs=[pl.BlockSpec(memory_space=pltpu.VMEM)] * len(arrays),
        out_specs=[pl.BlockSpec(memory_space=pltpu.HBM)] * len(arrays),
        out_shape=[pltpu.HBM(a.shape, a.dtype) for a in arrays],
        scratch_shapes=[pltpu.SemaphoreType.DMA((len(arrays),))],
        compiler_params=pltpu.CompilerParams(vmem_limit_bytes=4 * 1024 * 1024),
    )(*[pltpu.with_memory_space_constraint(a, pltpu.VMEM) for a in arrays])


def local(mesh_shape, signal, out_grad, residues, log_rates):
    batch_rows, length, channels = signal.shape
    modes, groups = log_rates.shape
    group = channels // groups
    n, rows = mesh_shape["seq"], mesh_shape["batch"]
    norm = 1.0 / (batch_rows * rows * length * n)
    forward, inverse, angle = constants(length)
    dft = np.asarray(forward).astype(jnp.bfloat16)
    dft = np.concatenate([dft, (forward - dft.astype(np.float32)).astype(jnp.bfloat16)], axis=1)
    inv_high = np.asarray(inverse).astype(jnp.bfloat16)
    inv_low = (inverse - inv_high.astype(np.float32)).astype(jnp.bfloat16)
    owner = np.arange(LANES)[None] // group == np.arange(LANES // group * modes)[:, None] // modes
    waves = np.stack(
        [dft] + [np.concatenate([v, v], axis=1) for v in (inv_high, inv_low)] + [owner.astype(jnp.bfloat16)]
    )
    half = channels // 2
    outer = n // 2
    count = half // (SUB * LANES)
    steps = 2 * count
    owners = min(outer, half // (rows * TILE))
    unit = half // (rows * owners)

    def dma(size):
        return pltpu.SemaphoreType.DMA((max(size, 1),))

    def vmem(*shape, dtype=F32):
        return pltpu.VMEM(shape, dtype)

    hbm_spec = pl.BlockSpec(memory_space=pltpu.HBM)
    vmem_spec = pl.BlockSpec(memory_space=pltpu.VMEM)
    links = [count, (outer - 1) * count, count, 1, rows * outer - 1, rows * n - 1, rows - 1, n - 1, rows, 1]
    mixed, grads, res_sum, rate_sum = [], [], 0.0, 0.0
    for row in range(batch_rows):
        held = (
            signal[row], out_grad[row], residues, log_rates, jnp.asarray(waves), jnp.asarray(angle)
        )
        y, gs, part, rates = pl.pallas_call(
            functools.partial(whole_kernel, n, rows, norm, modes, group, owners, plan_of(count)),
            in_specs=[hbm_spec] * 6,
            out_specs=[vmem_spec] * 4,
            out_shape=[
                vmem(length, channels, dtype=BF16),
                vmem(length, channels, dtype=BF16),
                vmem(modes, channels),
                vmem(modes, groups),
            ],
            scratch_shapes=[
                vmem(length, channels, dtype=BF16),
                vmem(length, channels, dtype=BF16),
                vmem(modes, channels),
                vmem(modes, groups),
                vmem(*waves.shape, dtype=BF16),
                vmem(*angle.shape),
                vmem(modes, groups),
                vmem(modes, groups),
                vmem(modes, groups),
                vmem(modes, channels),
                vmem(channels // LANES, modes, TILE),
                vmem(2, modes, channels),
                vmem(2, modes, channels),
                vmem(length, channels),
                vmem(length, channels),
                vmem(2, 2 * length, SUB * LANES, dtype=BF16),
                vmem(modes, channels),
                vmem(modes, channels),
                vmem(modes, half),
                vmem(2, modes, half),
                vmem(2, modes, half),
                vmem(2, modes, half),
                vmem(outer, modes, half),
                vmem(2, modes, half),
                vmem(2, modes, channels),
                vmem(modes, half),
                vmem(modes, half),
                vmem(max(rows * outer - 1, 1), modes, unit),
                vmem(rows, modes, groups),
                vmem(n, modes, groups),
                dma(2 * steps + 4),
            ]
            + [dma(size) for size in links for _ in range(2)],
            compiler_params=pltpu.CompilerParams(
                collective_id=0, has_side_effects=True, vmem_limit_bytes=32 * 1024 * 1024
            ),
        )(*[pltpu.with_memory_space_constraint(a, pltpu.HBM) for a in held])
        y, gs, part, rates = leave(y, gs, part, rates)
        mixed.append(y)
        grads.append(gs)
        res_sum = res_sum + part if row else part
        rate_sum = rate_sum + rates if row else rates
    return jnp.stack(mixed), jnp.stack(grads), res_sum, rate_sum


def solution(mesh):
    placed = (P("batch", "seq", None), P("batch", "seq", None), P(), P())
    return jax.shard_map(
        functools.partial(local, dict(mesh.shape)),
        mesh=mesh,
        in_specs=placed,
        out_specs=placed,
        check_vma=False,
    )
```

```python
import functools

import jax
import jax.numpy as jnp
import numpy as np
from jax import lax
from jax.experimental import pallas as pl
from jax.experimental.pallas import tpu as pltpu
from jax.sharding import PartitionSpec as P

LANES = 256
TILE = 128
SUB = 4
F32 = jnp.float32
BF16 = jnp.bfloat16
MESH = pl.DeviceIdType.MESH


def split(value):
    high = value.astype(BF16)
    return high, (value - high.astype(F32)).astype(BF16)


def mul(a, b):
    return jnp.dot(a, b, preferred_element_type=F32)


def twice(value, axis):
    return jnp.concatenate([value, value], axis=axis)


def own_rows(wide, modes, group):
    rows, lanes = wide.shape
    owner = lax.broadcasted_iota(jnp.int32, (modes, lanes), 1) // group
    out = wide[:modes]
    for g in range(1, rows // modes):
        out = jnp.where(owner == g, wide[g * modes : (g + 1) * modes], out)
    return out


def pick_lanes(tile, index):
    return jnp.take_along_axis(tile, index, axis=1, mode="promise_in_bounds")


def state_block(modes, group, rate, x, g):
    rows, length = rate.shape
    lane = lax.broadcasted_iota(jnp.int32, (rows, length), 1)
    at = lane.astype(F32)
    rising = jnp.exp(-rate * at)
    falling = pick_lanes(rising, length - 1 - lane)
    out = []
    for table, weight, values in ((falling, length - at, x), (rising, at, g)):
        left = jnp.concatenate([table, weight * table], axis=0)
        both = mul(jnp.concatenate(split(left), axis=1), twice(values, 0))
        out.append((own_rows(both[:rows], modes, group), own_rows(both[rows:], modes, group)))
    return out


def phi_of(pole, gap, angle):
    near = pole * angle[0]
    inverse = 1.0 / (gap * gap + (near + near))
    return (gap + near) * inverse, pole * angle[1] * inverse


def full(high, low):
    return jnp.concatenate([twice(high, 1), twice(low, 1)], axis=0)


def fold_rows(value):
    rows = value.shape[0] // 2
    return value[:rows] + value[rows:]


def lag_block(modes, group, pole, gap, angle, x_hat, g_hat):
    half = x_hat.shape[0] // 2
    r, i = phi_of(pole, gap, angle)
    lower = lax.broadcasted_iota(jnp.int32, r.shape, 1) < half
    terms = []
    for a, b in ((r, i), (r * r - i * i - r, 2.0 * r * i - i)):
        terms += [jnp.where(lower, a, pltpu.roll(b, half, 1)), jnp.where(lower, pltpu.roll(a, half, 1), b)]
    gm = 2 * r.shape[0]
    xr, xi = x_hat[:half], x_hat[half:]
    gr, gi = g_hat[:half], g_hat[half:]
    lag = jnp.concatenate([gr * xr + gi * xi, gr * xi - gi * xr], axis=0) * (1.0 / half)
    left = full(*split(jnp.concatenate(terms, axis=0)))
    wide = fold_rows(mul(left, jnp.concatenate(split(lag), axis=0)))
    return own_rows(wide[:gm], modes, group), own_rows(wide[gm:], modes, group)


def spread(narrow, mask):
    high, low = split(twice(narrow, 0))
    times = mask.shape[0] // high.shape[0]
    return jnp.concatenate(
        [jnp.concatenate([part] * times, axis=0) * mask for part in (high, low)], axis=0
    )


def hat_block(rate, mask, angle, x_hat, g_hat, res, start_x, start_g):
    half = x_hat.shape[0] // 2
    pole = jnp.exp(-rate)
    left = full(*split(jnp.concatenate(phi_of(pole, gap_of(rate), angle), axis=0)))
    right = jnp.concatenate([spread(v, mask) for v in (res, start_x, start_g)], axis=1)
    wide = fold_rows(mul(left, right))
    lanes = res.shape[1]
    (kr, ki), (cr, ci), (ar, ai) = [
        (wide[:half, at : at + lanes], wide[half:, at : at + lanes]) for at in (0, lanes, 2 * lanes)
    ]
    xr, xi = x_hat[:half], x_hat[half:]
    gr, gi = g_hat[:half], g_hat[half:]
    level = jnp.sum(start_g, axis=0, keepdims=True)
    y_hat = jnp.concatenate([kr * xr + ki * xi + cr, kr * xi - ki * xr - ci], axis=0)
    h_hat = jnp.concatenate([kr * gr - ki * gi + (level - ar), kr * gi + ki * gr - ai], axis=0)
    return jnp.concatenate(split(y_hat), axis=0), jnp.concatenate(split(h_hat), axis=0)


def gap_of(rate):
    gap = jnp.ones_like(rate)
    for k in range(7, 1, -1):
        gap = 1.0 - rate * gap * (1.0 / k)
    return rate * gap


def remote(source, target, sems, k, where):
    return pltpu.make_async_remote_copy(
        src_ref=source, dst_ref=target, send_sem=sems[0].at[k], recv_sem=sems[1].at[k],
        device_id=where, device_id_type=MESH,
    )


def whole_kernel(
    n, rows, norm, modes, group, owners, plan,
    x_hbm, g_hbm, res_hbm, log_hbm, waves_hbm, angle_hbm,
    y_ref, gs_ref, gathered_ref, grate_ref,
    x_ref, g_ref, res_ref, log_ref, waves_ref, angle_ref, decay_ref, pole_ref, gap_ref, rates_ref, rows_ref,
    state_ref, weighted_ref, x_hat_ref, g_hat_ref, hat_ref, sum_ref, moment_ref, cross_ref,
    pair_ref, weighted_pair_ref, total_ref, near_ref, joint_ref, outer_ref, back_ref, landed_ref, sum_pair_ref, owned_ref,
    reduced_ref, rate_row_ref, rate_seq_ref,
    in_sems, *sems,
):
    length, channels = x_ref.shape
    groups = log_ref.shape[1]
    half = channels // 2
    chunk = SUB * LANES
    count = half // chunk
    steps = 2 * count
    outer = n // 2
    me = lax.axis_index("seq")
    mine = lax.axis_index("batch")
    z, side = lax.div(me, 2), lax.rem(me, 2)
    two, odd, twos = lax.div(z, 2), lax.rem(z, 2), outer // 2
    own_base, pair_base = side * half, (1 - side) * half
    unit = half // (rows * owners)
    pairs = [(sems[2 * i], sems[2 * i + 1]) for i in range(len(sems) // 2)]
    partner = {"seq": me + 1 - 2 * side}

    def lanes(start, width=chunk):
        return pl.ds(pl.multiple_of(start, TILE), width)

    def base_of(j):
        return jnp.where(j < count, pair_base + j * chunk, own_base + (j - count) * chunk)

    def loads(j):
        here = lanes(base_of(j))
        return [
            pltpu.make_async_copy(x_hbm.at[:, here], x_ref.at[:, here], in_sems.at[j]),
            pltpu.make_async_copy(g_hbm.at[:, here], g_ref.at[:, here], in_sems.at[steps + j]),
        ]

    load_log = pltpu.make_async_copy(log_hbm, log_ref, in_sems.at[2 * steps])
    late = [
        pltpu.make_async_copy(source, target, in_sems.at[2 * steps + 1 + i])
        for i, (source, target) in enumerate(
            ((waves_hbm, waves_ref), (angle_hbm, angle_ref), (res_hbm, res_ref))
        )
    ]

    def to_pair(k):
        here = lanes(pair_base + k * chunk)
        return remote(
            state_ref.at[:, :, here], pair_ref.at[:, :, lanes(k * chunk)], pairs[0], k, partner
        )

    def weights_to_pair():
        return remote(
            weighted_ref.at[:, :, lanes(pair_base, half)], weighted_pair_ref, pairs[9], 0, partner
        )

    def to_near(k):
        here = lanes(k * chunk)
        return remote(
            total_ref.at[odd, :, here], near_ref.at[:, here], pairs[10], k,
            {"seq": 2 * (z + 1 - 2 * odd) + side},
        )

    def to_outer(k):
        here = lanes(k * chunk)
        out = []
        for q in range(twos):
            for m in range(2):
                wanted = jnp.where(odd == 1, q > two, q < two)
                out.append(
                    (
                        wanted,
                        pltpu.make_async_remote_copy(
                            src_ref=joint_ref.at[:, here], dst_ref=outer_ref.at[two, :, here],
                            send_sem=pairs[1][0].at[(2 * q + m) * count + k],
                            recv_sem=pairs[1][1].at[two * count + k],
                            device_id={"seq": 2 * (2 * q + m) + side}, device_id_type=MESH,
                        ),
                    )
                )
        return out

    def from_outer(k):
        here = lanes(k * chunk)
        return [
            (
                q != two,
                pltpu.make_async_remote_copy(
                    src_ref=joint_ref.at[:, here], dst_ref=outer_ref.at[q, :, here],
                    send_sem=pairs[1][0].at[2 * q * count + k], recv_sem=pairs[1][1].at[q * count + k],
                    device_id={"seq": 4 * q + side}, device_id_type=MESH,
                ),
            )
            for q in range(twos)
        ]

    def to_back(k):
        return remote(
            back_ref.at[:, :, lanes(k * chunk)], landed_ref.at[:, :, lanes(own_base + k * chunk)],
            pairs[2], k, partner,
        )

    def sums_to_pair():
        return remote(sum_ref.at[:, lanes(pair_base, half)], sum_pair_ref, pairs[3], 0, partner)

    def owned_at(q, zo):
        return q * (half // rows) + zo * unit

    def guarded(condition, action):
        if owners == outer:
            action()
        else:
            pl.when(condition)(action)

    near = [(q, i) for q in range(rows) for i in range(outer) if q or i]
    stride = 2 if rows % 2 == 0 else 1
    far = [(q, i) for q in range(0, rows, stride) for i in range(n) if q or i]
    known = [(q, i) for q in range(rows) for i in range(n) if (q or i) and (q % stride == 0 or i % 2 == 0)]

    def reduce_copy(k):
        q, i = near[k]
        peer_q, peer_z = lax.rem(mine + q, rows), lax.rem(z + i, outer)
        return peer_z, remote(
            owned_ref.at[:, lanes(owned_at(peer_q, jnp.minimum(peer_z, owners - 1)), unit)],
            reduced_ref.at[k], pairs[4], k, {"batch": peer_q, "seq": 2 * peer_z + side},
        )

    def gather_copy(k):
        q, i = far[k]
        here = lanes(own_base + owned_at(mine, jnp.minimum(z, owners - 1)), unit)
        return lax.div(lax.rem(me + n - i, n), 2), remote(
            gathered_ref.at[:, here], gathered_ref.at[:, here], pairs[5], k,
            {"batch": lax.rem(mine + q, rows), "seq": lax.rem(me + i, n)},
        )

    def spread_copies():
        if stride == 1:
            return []
        second = lax.rem(mine, 2)
        width = half // rows
        out = []
        for i in range(2):
            for t in range(rows // 2):
                here = lanes(i * half + (second + 2 * t) * width, width)
                out.append(
                    remote(
                        gathered_ref.at[:, here], gathered_ref.at[:, here], pairs[8],
                        i * (rows // 2) + t, {"batch": mine + 1 - 2 * second},
                    )
                )
        return out

    def rates_beside():
        return [
            remote(
                rate_row_ref.at[mine], rate_row_ref.at[mine], pairs[6], i - 1,
                {"batch": lax.rem(mine + i, rows)},
            )
            for i in range(1, rows)
        ]

    def rates_along():
        return [
            remote(
                rate_seq_ref.at[me], rate_seq_ref.at[me], pairs[7], i - 1,
                {"seq": lax.rem(me + i, n)},
            )
            for i in range(1, n)
        ]

    load_log.start()
    barrier = pltpu.get_barrier_semaphore()
    for copy in loads(0):
        copy.start()
    for q, i in known:
        pl.semaphore_signal(
            barrier, inc=1, device_id={"batch": lax.rem(mine + q, rows), "seq": lax.rem(me + i, n)},
            device_id_type=MESH,
        )
    for j in range(1, steps):
        for copy in loads(j):
            copy.start()
    for copy in late:
        copy.start()
    outer_ref[two] = jnp.zeros((modes, half), F32)

    load_log.wait()
    decay = jnp.exp(log_ref[...])
    decay_ref[...] = decay
    pole_ref[...] = jnp.exp(-decay)
    gap_ref[...] = gap_of(decay)
    per_block = LANES // group

    def tile_of(base, s):
        first = lax.div(base, group) + s * per_block
        return lanes(lax.div(first, TILE) * TILE, TILE), lax.rem(first, TILE)

    def states(j, nothing):
        base = base_of(j)
        for copy in loads(j):
            copy.wait()
        for s in range(SUB):
            at = lanes(base + s * LANES, LANES)
            tile, shift = tile_of(base, s)
            rate = jnp.concatenate(
                [
                    pick_lanes(decay_ref[:, tile], jnp.full((modes, TILE), shift + g))
                    for g in range(per_block)
                ],
                0,
            )
            (s_x, w_x), (s_g, w_g) = state_block(modes, group, rate, x_ref[:, at], g_ref[:, at])
            state_ref[0, :, at] = s_x
            state_ref[1, :, at] = s_g
            weighted_ref[0, :, at] = w_x
            weighted_ref[1, :, at] = w_g

        for k in range(count):
            @pl.when(j == k)
            def _():
                if k == 0:
                    pl.semaphore_wait(barrier, len(known))
                to_pair(k).start()

        return nothing

    lax.fori_loop(0, steps, states, 0)

    lane = lax.broadcasted_iota(jnp.int32, (modes, TILE), 1)
    sub = lax.broadcasted_iota(jnp.int32, (modes, TILE), 0)
    per_tile = TILE // group
    for k in range(channels // TILE):
        first = k * per_tile
        tile = decay_ref[:, first // TILE * TILE : (first // TILE + 1) * TILE]
        rates_ref[:, k * TILE : (k + 1) * TILE] = pick_lanes(tile, lane // group + first % TILE)
    for b in range(channels // LANES):
        first = b * per_block
        tile = decay_ref[:, first // TILE * TILE : (first // TILE + 1) * TILE]
        taken = pick_lanes(tile, lane // modes + first % TILE)
        row = jnp.sum(jnp.where(lane % modes == sub, taken, 0.0), axis=0, keepdims=True)
        rows_ref[b] = jnp.broadcast_to(row, (modes, TILE))

    def both_of(k):
        at, here = lanes(own_base + k * chunk), lanes(k * chunk)
        first = side == 0
        ours, theirs = [state_ref[i, :, at] for i in (0, 1)], [pair_ref[i, :, here] for i in (0, 1)]
        a = [jnp.where(first, o, t) for o, t in zip(ours, theirs)]
        b = [jnp.where(first, t, o) for o, t in zip(ours, theirs)]
        return a, b, jnp.exp(-rates_ref[:, at] * float(length)), first, at, here

    def send_total(k):
        to_pair(k).wait_recv()
        a, b, whole, first, at, here = both_of(k)
        total_ref[0, :, here] = whole * a[0] + b[0]
        total_ref[1, :, here] = a[1] + whole * b[1]
        to_near(k).start()

    def send_joint(k):
        to_near(k).wait_recv()
        here = lanes(k * chunk)
        whole = jnp.exp(-rates_ref[:, lanes(own_base + k * chunk)] * float(length))
        joint_ref[:, here] = whole * whole * near_ref[:, here] + total_ref[1 - odd, :, here]
        for wanted, copy in to_outer(k):
            pl.when(wanted)(copy.start)

    def take_total(k):
        for wanted, copy in from_outer(k):
            pl.when(wanted)(copy.wait_recv)
        a, b, whole, first, at, here = both_of(k)
        twofold = whole * whole
        fourfold = twofold * twofold
        carry = jnp.zeros_like(whole)
        adjoint = jnp.zeros_like(whole)
        for i in range(twos):
            carry = jnp.where(i < two, outer_ref[i, :, here] + fourfold * carry, carry)
            last = twos - 1 - i
            adjoint = jnp.where(last > two, outer_ref[last, :, here] + fourfold * adjoint, adjoint)
        beside = near_ref[:, here]
        carry = jnp.where(odd == 1, beside + twofold * carry, carry)
        adjoint = jnp.where(odd == 1, adjoint, beside + twofold * adjoint)
        carry_b = whole * carry + a[0]
        adjoint_a = whole * adjoint + b[1]
        back_ref[0, :, here] = jnp.where(first, carry_b, carry)
        back_ref[1, :, here] = jnp.where(first, adjoint, adjoint_a)
        to_back(k).start()
        landed_ref[0, :, at] = jnp.where(first, carry, carry_b)
        landed_ref[1, :, at] = jnp.where(first, adjoint_a, adjoint)
        if k == 0:
            weights_to_pair().wait_recv()
        ours = [weighted_ref[i, :, at] for i in (0, 1)]
        theirs = [weighted_pair_ref[i, :, here] for i in (0, 1)]
        cross, moments = jnp.zeros_like(whole), jnp.zeros_like(whole)
        for (s_x, s_g), (w_x, w_g), into, back in (
            (a, [jnp.where(first, o, t) for o, t in zip(ours, theirs)], carry, adjoint_a),
            (b, [jnp.where(first, t, o) for o, t in zip(ours, theirs)], carry_b, adjoint),
        ):
            turned_x, turned_g = s_x / (1.0 + whole), s_g / (1.0 + whole)
            into_all = into + turned_x
            cross += into_all * s_g
            moments += (into_all * w_g + (back + turned_g) * w_x) + float(length) * whole * (
                into * back - turned_x * turned_g
            )
        rate = rates_ref[:, at]
        pole = jnp.exp(-rate)
        owned_ref[:, here] = pole * cross
        cross_ref[:, here] = -rate * res_ref[:, at] * pole * moments

    def group_sums(value):
        parts = [value[:, t * TILE : (t + 1) * TILE] for t in range(value.shape[1] // TILE)]
        many, shift = len(parts), 1
        while shift < group:
            if len(parts) > 1:
                low = (lane & shift) == 0
                parts = [
                    jnp.where(low, a, b) + pick_lanes(jnp.where(low, b, a), lane ^ shift)
                    for a, b in zip(parts[::2], parts[1::2])
                ]
            else:
                parts = [parts[0] + pick_lanes(parts[0], lane ^ shift)]
            shift *= 2
        return pick_lanes(parts[0], lane % per_tile * group + lane // per_tile % many)

    def start_reduce(nothing):
        sums_to_pair().wait_recv()
        owned_ref[...] = owned_ref[...] + (sum_ref[:, lanes(own_base, half)] + sum_pair_ref[...])
        for k in range(len(near)):
            peer_z, copy = reduce_copy(k)
            guarded(peer_z < owners, copy.start)

    def start_rates(nothing):
        own = lanes(own_base, half)
        moment_ref[:, own] = moment_ref[:, own] + cross_ref[...]
        held = TILE * group // chunk
        for t in range(groups // TILE):
            out = jnp.zeros((modes, TILE), F32)
            for i in range(held):
                base = (t * held + i) * chunk
                sums = group_sums(moment_ref[:, base : base + chunk])
                out = jnp.where(lane // (TILE // held) == i, sums, out)
            rate_row_ref[mine, :, t * TILE : (t + 1) * TILE] = out
        for copy in rates_beside():
            copy.start()

    def start_gather(nothing):
        own_at = owned_at(mine, jnp.minimum(z, owners - 1))

        def finish_reduce():
            part = owned_ref[:, lanes(own_at, unit)]
            for k in range(len(near)):
                reduce_copy(k)[1].wait_recv()
                part = part + reduced_ref[k]
            gathered_ref[:, lanes(own_base + own_at, unit)] = part * norm
            for k in range(len(far)):
                gather_copy(k)[1].start()

        guarded(z < owners, finish_reduce)

    def start_along(nothing):
        for copy in rates_beside():
            copy.wait_recv()
        part = rate_row_ref[0]
        for i in range(1, rows):
            part = part + rate_row_ref[i]
        rate_seq_ref[me] = part
        for copy in rates_along():
            copy.start()

    events = {
        "total": send_total, "joint": send_joint, "take": take_total, "reduce": start_reduce, "gather": start_gather,
        "rates": start_rates, "along": start_along,
        "back": lambda k: to_back(k).wait_recv(), "sums": lambda k: sums_to_pair().start(),
    }

    def run_events(phase, j):
        for step, name, k in plan[phase]:
            @pl.when(j == step)
            def _():
                events[name](k)

    def lags(j, nothing):
        run_events("lags", j)
        base = base_of(j)
        here = lanes(base)
        x_hat_ref[:, here] = mul(waves_ref[0], twice(x_ref[:, here], 0))
        g_hat_ref[:, here] = mul(waves_ref[0], twice(g_ref[:, here], 0))
        for s in range(SUB):
            at = lanes(base + s * LANES, LANES)
            tile, shift = tile_of(base, s)
            upper = jnp.where(lane < length // 2, shift, shift + per_block // 2)
            pole, gap = [
                jnp.concatenate(
                    [pick_lanes(ref[:, tile], upper + g) for g in range(per_block // 2)], 0
                )
                for ref in (pole_ref, gap_ref)
            ]
            sums, moments = lag_block(
                modes, group, pole, gap, angle_ref[:, length // 2 :][:, :1],
                x_hat_ref[:, at], g_hat_ref[:, at],
            )
            sum_ref[:, at] = sums
            moment_ref[:, at] = -rates_ref[:, at] * res_ref[:, at] * moments
        return nothing

    for copy in late:
        copy.wait()
    weights_to_pair().start()
    send_total(0)
    lax.fori_loop(0, steps, lags, 0)

    order = plan["order"]

    def base_out(j):
        base = own_base
        for i, (own, k) in enumerate(order):
            base = jnp.where(j == i, (own_base if own else pair_base) + k * chunk, base)
        return base

    def outs(j, nothing):
        run_events("outs", j)
        base = base_out(j)
        for s in range(SUB):
            at = lanes(base + s * LANES, LANES)
            rate = rows_ref[lax.div(base, LANES) + s, 0:1, :]
            res = res_ref[:, at]
            pole = jnp.exp(-rates_ref[:, at])
            above = 1.0 + jnp.exp(-rates_ref[:, at] * float(length))
            start_x = res * pole * (above * landed_ref[0, :, at] + state_ref[0, :, at])
            start_g = res * (above * landed_ref[1, :, at] + state_ref[1, :, at])
            y_hat, h_hat = hat_block(
                rate, waves_ref[3], angle_ref[:, : length // 2],
                x_hat_ref[:, at], g_hat_ref[:, at], res, start_x, start_g,
            )
            hat_ref[0, :, s * LANES : (s + 1) * LANES] = y_hat
            hat_ref[1, :, s * LANES : (s + 1) * LANES] = h_hat
        inverse = jnp.concatenate([waves_ref[1], waves_ref[2]], axis=0)
        here = lanes(base)
        y_ref[:, here] = fold_rows(mul(inverse, hat_ref[0])).astype(BF16)
        gs_ref[:, here] = fold_rows(mul(inverse, hat_ref[1])).astype(BF16)
        return nothing

    lax.fori_loop(0, steps, outs, 0)

    for k in range(len(far)):
        from_z, copy = gather_copy(k)
        guarded(from_z < owners, copy.wait_recv)
    for copy in spread_copies():
        copy.start()
    for copy in rates_along():
        copy.wait_recv()
    part = rate_seq_ref[0]
    for i in range(1, n):
        part = part + rate_seq_ref[i]
    grate_ref[...] = part * norm
    for copy in spread_copies():
        copy.wait_recv()

    for k in range(count):
        for copy in [to_pair(k), to_back(k), to_near(k)]:
            copy.wait_send()
        for wanted, copy in to_outer(k):
            pl.when(wanted)(copy.wait_send)
    sums_to_pair().wait_send()
    weights_to_pair().wait_send()
    for k in range(len(near)):
        peer_z, copy = reduce_copy(k)
        guarded(peer_z < owners, copy.wait_send)
    for k in range(len(far)):
        guarded(z < owners, gather_copy(k)[1].wait_send)
    for copy in rates_beside() + rates_along() + spread_copies():
        copy.wait_send()


def constants(length):
    half = length // 2
    omega = np.pi * (2.0 * np.arange(half) + 1.0) / length
    at = np.arange(length)
    forward = np.concatenate([np.cos(np.outer(omega, at)), -np.sin(np.outer(omega, at))], axis=0)
    parts = np.stack([2.0 * np.sin(omega / 2.0) ** 2, np.sin(omega)])
    angle = np.concatenate(
        [
            np.broadcast_to(parts[:, :, None], (2, half, 2 * half)),
            np.broadcast_to(np.tile(parts, (1, 2))[:, None], (2, 8, 2 * half)),
        ],
        axis=1,
    )
    return forward.astype(np.float32), (forward.T / half).astype(np.float32), angle.astype(np.float32)


def plan_of(count):
    last = 2 * count - 1
    own = [(True, k) for k in range(count)]
    pair = [(False, k) for k in range(count)]
    order = own[:2] + [v for both in zip(pair, own[2:] + [None] * 2) for v in both if v]
    lags = [(t, "total", k + 1) for k, t in enumerate([0, 1, 2])] + [(count, "sums", 0)]
    lags += [(t, "joint", k) for k, t in enumerate([3, 4, 5, 6])]
    lags += [(t, "take", k) for k, t in enumerate([7])]
    outs = [(t, "take", k + 1) for k, t in enumerate([0, 0, 1])]
    outs += [(1, "reduce", 0), (1, "rates", 0), (4, "gather", 0), (5, "along", 0)]
    outs += [(order.index(v), "back", v[1]) for v in pair]
    return {"lags": lags, "outs": outs, "order": order}


def leave_kernel(*refs):
    count = len(refs) // 2
    sems = refs[-1]
    copies = []
    for i, (source, target) in enumerate(zip(refs[:count], refs[count:])):
        copies.append(pltpu.make_async_copy(source, target, sems.at[i]))
    for copy in copies:
        copy.start()
    for copy in copies:
        copy.wait()


def leave(*arrays):
    return pl.pallas_call(
        leave_kernel,
        in_specs=[pl.BlockSpec(memory_space=pltpu.VMEM)] * len(arrays),
        out_specs=[pl.BlockSpec(memory_space=pltpu.HBM)] * len(arrays),
        out_shape=[pltpu.HBM(a.shape, a.dtype) for a in arrays],
        scratch_shapes=[pltpu.SemaphoreType.DMA((len(arrays),))],
        compiler_params=pltpu.CompilerParams(vmem_limit_bytes=4 * 1024 * 1024),
    )(*[pltpu.with_memory_space_constraint(a, pltpu.VMEM) for a in arrays])


def local(mesh_shape, signal, out_grad, residues, log_rates):
    batch_rows, length, channels = signal.shape
    modes, groups = log_rates.shape
    group = channels // groups
    n, rows = mesh_shape["seq"], mesh_shape["batch"]
    norm = 1.0 / (batch_rows * rows * length * n)
    forward, inverse, angle = constants(length)
    dft = np.asarray(forward).astype(jnp.bfloat16)
    dft = np.concatenate([dft, (forward - dft.astype(np.float32)).astype(jnp.bfloat16)], axis=1)
    inv_high = np.asarray(inverse).astype(jnp.bfloat16)
    inv_low = (inverse - inv_high.astype(np.float32)).astype(jnp.bfloat16)
    owner = np.arange(LANES)[None] // group == np.arange(LANES // group * modes)[:, None] // modes
    waves = np.stack(
        [dft] + [np.concatenate([v, v], axis=1) for v in (inv_high, inv_low)] + [owner.astype(jnp.bfloat16)]
    )
    half = channels // 2
    outer = n // 2
    count = half // (SUB * LANES)
    steps = 2 * count
    owners = min(outer, half // (rows * TILE))
    unit = half // (rows * owners)

    def dma(size):
        return pltpu.SemaphoreType.DMA((max(size, 1),))

    def vmem(*shape, dtype=F32):
        return pltpu.VMEM(shape, dtype)

    hbm_spec = pl.BlockSpec(memory_space=pltpu.HBM)
    vmem_spec = pl.BlockSpec(memory_space=pltpu.VMEM)
    links = [count, outer * count, count, 1, rows * outer - 1, rows * n - 1, rows - 1, n - 1, rows, 1, count]
    mixed, grads, res_sum, rate_sum = [], [], 0.0, 0.0
    for row in range(batch_rows):
        held = (
            signal[row], out_grad[row], residues, log_rates, jnp.asarray(waves), jnp.asarray(angle)
        )
        y, gs, part, rates = pl.pallas_call(
            functools.partial(whole_kernel, n, rows, norm, modes, group, owners, plan_of(count)),
            in_specs=[hbm_spec] * 6,
            out_specs=[vmem_spec] * 4,
            out_shape=[
                vmem(length, channels, dtype=BF16),
                vmem(length, channels, dtype=BF16),
                vmem(modes, channels),
                vmem(modes, groups),
            ],
            scratch_shapes=[
                vmem(length, channels, dtype=BF16),
                vmem(length, channels, dtype=BF16),
                vmem(modes, channels),
                vmem(modes, groups),
                vmem(*waves.shape, dtype=BF16),
                vmem(*angle.shape),
                vmem(modes, groups),
                vmem(modes, groups),
                vmem(modes, groups),
                vmem(modes, channels),
                vmem(channels // LANES, modes, TILE),
                vmem(2, modes, channels),
                vmem(2, modes, channels),
                vmem(length, channels),
                vmem(length, channels),
                vmem(2, 2 * length, SUB * LANES, dtype=BF16),
                vmem(modes, channels),
                vmem(modes, channels),
                vmem(modes, half),
                vmem(2, modes, half),
                vmem(2, modes, half),
                vmem(2, modes, half),
                vmem(modes, half),
                vmem(modes, half),
                vmem(outer // 2, modes, half),
                vmem(2, modes, half),
                vmem(2, modes, channels),
                vmem(modes, half),
                vmem(modes, half),
                vmem(max(rows * outer - 1, 1), modes, unit),
                vmem(rows, modes, groups),
                vmem(n, modes, groups),
                dma(2 * steps + 4),
            ]
            + [dma(size) for size in links for _ in range(2)],
            compiler_params=pltpu.CompilerParams(
                collective_id=0, has_side_effects=True, vmem_limit_bytes=32 * 1024 * 1024
            ),
        )(*[pltpu.with_memory_space_constraint(a, pltpu.HBM) for a in held])
        y, gs, part, rates = leave(y, gs, part, rates)
        mixed.append(y)
        grads.append(gs)
        res_sum = res_sum + part if row else part
        rate_sum = rate_sum + rates if row else rates
    return jnp.stack(mixed), jnp.stack(grads), res_sum, rate_sum


def solution(mesh):
    placed = (P("batch", "seq", None), P("batch", "seq", None), P(), P())
    return jax.shard_map(
        functools.partial(local, dict(mesh.shape)),
        mesh=mesh,
        in_specs=placed,
        out_specs=placed,
        check_vma=False,
    )
```

```python
import functools

import jax
import jax.numpy as jnp
import numpy as np
from jax import lax
from jax.experimental import pallas as pl
from jax.experimental.pallas import tpu as pltpu
from jax.sharding import PartitionSpec as P

LANES = 256
TILE = 128
SUB = 4
F32 = jnp.float32
BF16 = jnp.bfloat16
MESH = pl.DeviceIdType.MESH


def split(value):
    high = value.astype(BF16)
    return high, (value - high.astype(F32)).astype(BF16)


def mul(a, b):
    return jnp.dot(a, b, preferred_element_type=F32)


def twice(value, axis):
    return jnp.concatenate([value, value], axis=axis)


def own_rows(wide, modes, group):
    rows, lanes = wide.shape
    owner = lax.broadcasted_iota(jnp.int32, (modes, lanes), 1) // group
    out = wide[:modes]
    for g in range(1, rows // modes):
        out = jnp.where(owner == g, wide[g * modes : (g + 1) * modes], out)
    return out


def pick_lanes(tile, index):
    return jnp.take_along_axis(tile, index, axis=1, mode="promise_in_bounds")


def state_block(modes, group, rate, x, g):
    rows, length = rate.shape
    lane = lax.broadcasted_iota(jnp.int32, (rows, length), 1)
    at = lane.astype(F32)
    rising = jnp.exp(-rate * at)
    falling = pick_lanes(rising, length - 1 - lane)
    out = []
    for table, weight, values in ((falling, length - at, x), (rising, at, g)):
        left = jnp.concatenate([table, weight * table], axis=0)
        both = mul(jnp.concatenate(split(left), axis=1), twice(values, 0))
        out.append((own_rows(both[:rows], modes, group), own_rows(both[rows:], modes, group)))
    return out


def phi_of(pole, gap, angle):
    near = pole * angle[0]
    inverse = 1.0 / (gap * gap + (near + near))
    return (gap + near) * inverse, pole * angle[1] * inverse


def full(high, low):
    return jnp.concatenate([twice(high, 1), twice(low, 1)], axis=0)


def fold_rows(value):
    rows = value.shape[0] // 2
    return value[:rows] + value[rows:]


def lag_block(modes, group, pole, gap, angle, x_hat, g_hat):
    half = x_hat.shape[0] // 2
    r, i = phi_of(pole, gap, angle)
    lower = lax.broadcasted_iota(jnp.int32, r.shape, 1) < half
    terms = []
    for a, b in ((r, i), (r * r - i * i - r, 2.0 * r * i - i)):
        terms += [jnp.where(lower, a, pltpu.roll(b, half, 1)), jnp.where(lower, pltpu.roll(a, half, 1), b)]
    gm = 2 * r.shape[0]
    xr, xi = x_hat[:half], x_hat[half:]
    gr, gi = g_hat[:half], g_hat[half:]
    lag = jnp.concatenate([gr * xr + gi * xi, gr * xi - gi * xr], axis=0) * (1.0 / half)
    left = full(*split(jnp.concatenate(terms, axis=0)))
    wide = fold_rows(mul(left, jnp.concatenate(split(lag), axis=0)))
    return own_rows(wide[:gm], modes, group), own_rows(wide[gm:], modes, group)


def spread(narrow, mask):
    high, low = split(twice(narrow, 0))
    times = mask.shape[0] // high.shape[0]
    return jnp.concatenate(
        [jnp.concatenate([part] * times, axis=0) * mask for part in (high, low)], axis=0
    )


def hat_block(rate, mask, angle, x_hat, g_hat, res, start_x, start_g):
    half = x_hat.shape[0] // 2
    pole = jnp.exp(-rate)
    left = full(*split(jnp.concatenate(phi_of(pole, gap_of(rate), angle), axis=0)))
    right = jnp.concatenate([spread(v, mask) for v in (res, start_x, start_g)], axis=1)
    wide = fold_rows(mul(left, right))
    lanes = res.shape[1]
    (kr, ki), (cr, ci), (ar, ai) = [
        (wide[:half, at : at + lanes], wide[half:, at : at + lanes]) for at in (0, lanes, 2 * lanes)
    ]
    xr, xi = x_hat[:half], x_hat[half:]
    gr, gi = g_hat[:half], g_hat[half:]
    level = jnp.sum(start_g, axis=0, keepdims=True)
    y_hat = jnp.concatenate([kr * xr + ki * xi + cr, kr * xi - ki * xr - ci], axis=0)
    h_hat = jnp.concatenate([kr * gr - ki * gi + (level - ar), kr * gi + ki * gr - ai], axis=0)
    return jnp.concatenate(split(y_hat), axis=0), jnp.concatenate(split(h_hat), axis=0)


def gap_of(rate):
    gap = jnp.ones_like(rate)
    for k in range(7, 1, -1):
        gap = 1.0 - rate * gap * (1.0 / k)
    return rate * gap


def remote(source, target, sems, k, where):
    return pltpu.make_async_remote_copy(
        src_ref=source, dst_ref=target, send_sem=sems[0].at[k], recv_sem=sems[1].at[k],
        device_id=where, device_id_type=MESH,
    )


def whole_kernel(
    n, rows, norm, modes, group, owners, plan,
    x_hbm, g_hbm, res_hbm, log_hbm, waves_hbm, angle_hbm,
    y_ref, gs_ref, gathered_ref, grate_ref,
    x_ref, g_ref, res_ref, log_ref, waves_ref, angle_ref, decay_ref, pole_ref, gap_ref, rates_ref, poles_ref, whole_ref, fold_ref, rows_ref,
    state_ref, weighted_ref, x_hat_ref, g_hat_ref, hat_ref, sum_ref, moment_ref, cross_ref,
    pair_ref, weighted_pair_ref, total_ref, near_ref, joint_ref, outer_ref, back_ref, landed_ref, sum_pair_ref, owned_ref,
    reduced_ref, rate_row_ref, rate_seq_ref,
    in_sems, *sems,
):
    length, channels = x_ref.shape
    groups = log_ref.shape[1]
    half = channels // 2
    chunk = SUB * LANES
    count = half // chunk
    steps = 2 * count
    outer = n // 2
    me = lax.axis_index("seq")
    mine = lax.axis_index("batch")
    z, side = lax.div(me, 2), lax.rem(me, 2)
    two, odd, twos = lax.div(z, 2), lax.rem(z, 2), outer // 2
    own_base, pair_base = side * half, (1 - side) * half
    unit = half // (rows * owners)
    pairs = [(sems[2 * i], sems[2 * i + 1]) for i in range(len(sems) // 2)]
    partner = {"seq": me + 1 - 2 * side}

    def lanes(start, width=chunk):
        return pl.ds(pl.multiple_of(start, TILE), width)

    def base_of(j):
        return jnp.where(j < count, pair_base + j * chunk, own_base + (j - count) * chunk)

    def loads(j):
        here = lanes(base_of(j))
        return [
            pltpu.make_async_copy(x_hbm.at[:, here], x_ref.at[:, here], in_sems.at[j]),
            pltpu.make_async_copy(g_hbm.at[:, here], g_ref.at[:, here], in_sems.at[steps + j]),
        ]

    load_log = pltpu.make_async_copy(log_hbm, log_ref, in_sems.at[2 * steps])
    late = [
        pltpu.make_async_copy(source, target, in_sems.at[2 * steps + 1 + i])
        for i, (source, target) in enumerate(
            ((waves_hbm, waves_ref), (angle_hbm, angle_ref), (res_hbm, res_ref))
        )
    ]

    def to_pair(k):
        here = lanes(pair_base + k * chunk)
        return remote(
            state_ref.at[:, :, here], pair_ref.at[:, :, lanes(k * chunk)], pairs[0], k, partner
        )

    def weights_to_pair():
        return remote(
            weighted_ref.at[:, :, lanes(pair_base, half)], weighted_pair_ref, pairs[9], 0, partner
        )

    def to_near(k):
        here = lanes(k * chunk)
        return remote(
            total_ref.at[odd, :, here], near_ref.at[:, here], pairs[10], k,
            {"seq": 2 * (z + 1 - 2 * odd) + side},
        )

    def to_outer(k):
        here = lanes(k * chunk)
        out = []
        for q in range(twos):
            for m in range(2):
                wanted = jnp.where(odd == 1, q > two, q < two)
                out.append(
                    (
                        wanted,
                        pltpu.make_async_remote_copy(
                            src_ref=joint_ref.at[:, here], dst_ref=outer_ref.at[two, :, here],
                            send_sem=pairs[1][0].at[(2 * q + m) * count + k],
                            recv_sem=pairs[1][1].at[two * count + k],
                            device_id={"seq": 2 * (2 * q + m) + side}, device_id_type=MESH,
                        ),
                    )
                )
        return out

    def from_outer(k):
        here = lanes(k * chunk)
        return [
            (
                q != two,
                pltpu.make_async_remote_copy(
                    src_ref=joint_ref.at[:, here], dst_ref=outer_ref.at[q, :, here],
                    send_sem=pairs[1][0].at[2 * q * count + k], recv_sem=pairs[1][1].at[q * count + k],
                    device_id={"seq": 4 * q + side}, device_id_type=MESH,
                ),
            )
            for q in range(twos)
        ]

    def to_back(k):
        return remote(
            back_ref.at[:, :, lanes(k * chunk)], landed_ref.at[:, :, lanes(own_base + k * chunk)],
            pairs[2], k, partner,
        )

    def sums_to_pair():
        return remote(sum_ref.at[:, lanes(pair_base, half)], sum_pair_ref, pairs[3], 0, partner)

    def owned_at(q, zo):
        return q * (half // rows) + zo * unit

    def guarded(condition, action):
        if owners == outer:
            action()
        else:
            pl.when(condition)(action)

    near = [(q, i) for q in range(rows) for i in range(outer) if q or i]
    stride = 2 if rows % 2 == 0 else 1
    far = [(q, i) for q in range(0, rows, stride) for i in range(n) if q or i]
    known = [(q, i) for q in range(rows) for i in range(n) if (q or i) and (q % stride == 0 or i % 2 == 0)]

    def reduce_copy(k):
        q, i = near[k]
        peer_q, peer_z = lax.rem(mine + q, rows), lax.rem(z + i, outer)
        return peer_z, remote(
            owned_ref.at[:, lanes(owned_at(peer_q, jnp.minimum(peer_z, owners - 1)), unit)],
            reduced_ref.at[k], pairs[4], k, {"batch": peer_q, "seq": 2 * peer_z + side},
        )

    def gather_copy(k):
        q, i = far[k]
        here = lanes(own_base + owned_at(mine, jnp.minimum(z, owners - 1)), unit)
        return lax.div(lax.rem(me + n - i, n), 2), remote(
            gathered_ref.at[:, here], gathered_ref.at[:, here], pairs[5], k,
            {"batch": lax.rem(mine + q, rows), "seq": lax.rem(me + i, n)},
        )

    def spread_copies():
        if stride == 1:
            return []
        second = lax.rem(mine, 2)
        width = half // rows
        out = []
        for i in range(2):
            for t in range(rows // 2):
                here = lanes(i * half + (second + 2 * t) * width, width)
                out.append(
                    remote(
                        gathered_ref.at[:, here], gathered_ref.at[:, here], pairs[8],
                        i * (rows // 2) + t, {"batch": mine + 1 - 2 * second},
                    )
                )
        return out

    def rates_beside():
        return [
            remote(
                rate_row_ref.at[mine], rate_row_ref.at[mine], pairs[6], i - 1,
                {"batch": lax.rem(mine + i, rows)},
            )
            for i in range(1, rows)
        ]

    def rates_along():
        return [
            remote(
                rate_seq_ref.at[me], rate_seq_ref.at[me], pairs[7], i - 1,
                {"seq": lax.rem(me + i, n)},
            )
            for i in range(1, n)
        ]

    load_log.start()
    barrier = pltpu.get_barrier_semaphore()
    for copy in loads(0):
        copy.start()
    for q, i in known:
        pl.semaphore_signal(
            barrier, inc=1, device_id={"batch": lax.rem(mine + q, rows), "seq": lax.rem(me + i, n)},
            device_id_type=MESH,
        )
    for j in range(1, steps):
        for copy in loads(j):
            copy.start()
    for copy in late:
        copy.start()
    outer_ref[two] = jnp.zeros((modes, half), F32)

    load_log.wait()
    decay = jnp.exp(log_ref[...])
    decay_ref[...] = decay
    pole_ref[...] = jnp.exp(-decay)
    gap_ref[...] = gap_of(decay)
    per_block = LANES // group

    lane = lax.broadcasted_iota(jnp.int32, (modes, TILE), 1)
    sub = lax.broadcasted_iota(jnp.int32, (modes, TILE), 0)
    per_tile = TILE // group
    for k in range(channels // TILE):
        first = k * per_tile
        tile = decay_ref[:, first // TILE * TILE : (first // TILE + 1) * TILE]
        here = slice(k * TILE, (k + 1) * TILE)
        rate = pick_lanes(tile, lane // group + first % TILE)
        whole = jnp.exp(-rate * float(length))
        rates_ref[:, here] = rate
        poles_ref[:, here] = jnp.exp(-rate)
        whole_ref[:, here] = whole
        fold_ref[:, here] = 1.0 / (1.0 + whole)
    for b in range(channels // LANES):
        first = b * per_block
        tile = decay_ref[:, first // TILE * TILE : (first // TILE + 1) * TILE]
        taken = pick_lanes(tile, lane // modes + first % TILE)
        row = jnp.sum(jnp.where(lane % modes == sub, taken, 0.0), axis=0, keepdims=True)
        rows_ref[b] = jnp.broadcast_to(row, (modes, TILE))

    def tile_of(base, s):
        first = lax.div(base, group) + s * per_block
        return lanes(lax.div(first, TILE) * TILE, TILE), lax.rem(first, TILE)

    def states(j, nothing):
        base = base_of(j)
        for copy in loads(j):
            copy.wait()
        for s in range(SUB):
            at = lanes(base + s * LANES, LANES)
            tile, shift = tile_of(base, s)
            rate = jnp.concatenate(
                [
                    pick_lanes(decay_ref[:, tile], jnp.full((modes, TILE), shift + g))
                    for g in range(per_block)
                ],
                0,
            )
            (s_x, w_x), (s_g, w_g) = state_block(modes, group, rate, x_ref[:, at], g_ref[:, at])
            state_ref[0, :, at] = s_x
            state_ref[1, :, at] = s_g
            weighted_ref[0, :, at] = w_x
            weighted_ref[1, :, at] = w_g

        for k in range(count):
            @pl.when(j == k)
            def _():
                if k == 0:
                    pl.semaphore_wait(barrier, len(known))
                to_pair(k).start()

        return nothing

    lax.fori_loop(0, steps, states, 0)

    def both_of(k):
        at, here = lanes(own_base + k * chunk), lanes(k * chunk)
        first = side == 0
        ours, theirs = [state_ref[i, :, at] for i in (0, 1)], [pair_ref[i, :, here] for i in (0, 1)]
        a = [jnp.where(first, o, t) for o, t in zip(ours, theirs)]
        b = [jnp.where(first, t, o) for o, t in zip(ours, theirs)]
        return a, b, whole_ref[:, at], first, at, here

    def send_total(k):
        to_pair(k).wait_recv()
        a, b, whole, first, at, here = both_of(k)
        total_ref[0, :, here] = whole * a[0] + b[0]
        total_ref[1, :, here] = a[1] + whole * b[1]
        to_near(k).start()

    def send_joint(k):
        to_near(k).wait_recv()
        here = lanes(k * chunk)
        whole = whole_ref[:, lanes(own_base + k * chunk)]
        joint_ref[:, here] = whole * whole * near_ref[:, here] + total_ref[1 - odd, :, here]
        for wanted, copy in to_outer(k):
            pl.when(wanted)(copy.start)

    def take_total(k):
        for wanted, copy in from_outer(k):
            pl.when(wanted)(copy.wait_recv)
        a, b, whole, first, at, here = both_of(k)
        twofold = whole * whole
        fourfold = twofold * twofold
        carry = jnp.zeros_like(whole)
        adjoint = jnp.zeros_like(whole)
        for i in range(twos):
            carry = jnp.where(i < two, outer_ref[i, :, here] + fourfold * carry, carry)
            last = twos - 1 - i
            adjoint = jnp.where(last > two, outer_ref[last, :, here] + fourfold * adjoint, adjoint)
        beside = near_ref[:, here]
        carry = jnp.where(odd == 1, beside + twofold * carry, carry)
        adjoint = jnp.where(odd == 1, adjoint, beside + twofold * adjoint)
        carry_b = whole * carry + a[0]
        adjoint_a = whole * adjoint + b[1]
        back_ref[0, :, here] = jnp.where(first, carry_b, carry)
        back_ref[1, :, here] = jnp.where(first, adjoint, adjoint_a)
        to_back(k).start()
        landed_ref[0, :, at] = jnp.where(first, carry, carry_b)
        landed_ref[1, :, at] = jnp.where(first, adjoint_a, adjoint)
        if k == 0:
            weights_to_pair().wait_recv()
        ours = [weighted_ref[i, :, at] for i in (0, 1)]
        theirs = [weighted_pair_ref[i, :, here] for i in (0, 1)]
        cross, moments, fold = jnp.zeros_like(whole), jnp.zeros_like(whole), fold_ref[:, at]
        for (s_x, s_g), (w_x, w_g), into, back in (
            (a, [jnp.where(first, o, t) for o, t in zip(ours, theirs)], carry, adjoint_a),
            (b, [jnp.where(first, t, o) for o, t in zip(ours, theirs)], carry_b, adjoint),
        ):
            turned_x, turned_g = s_x * fold, s_g * fold
            into_all = into + turned_x
            cross += into_all * s_g
            moments += (into_all * w_g + (back + turned_g) * w_x) + float(length) * whole * (
                into * back - turned_x * turned_g
            )
        rate, pole = rates_ref[:, at], poles_ref[:, at]
        owned_ref[:, here] = pole * cross
        cross_ref[:, here] = -rate * res_ref[:, at] * pole * moments

    def group_sums(value):
        parts = [value[:, t * TILE : (t + 1) * TILE] for t in range(value.shape[1] // TILE)]
        many, shift = len(parts), 1
        while shift < group:
            if len(parts) > 1:
                low = (lane & shift) == 0
                parts = [
                    jnp.where(low, a, b) + pick_lanes(jnp.where(low, b, a), lane ^ shift)
                    for a, b in zip(parts[::2], parts[1::2])
                ]
            else:
                parts = [parts[0] + pick_lanes(parts[0], lane ^ shift)]
            shift *= 2
        return pick_lanes(parts[0], lane % per_tile * group + lane // per_tile % many)

    def start_reduce(nothing):
        sums_to_pair().wait_recv()
        owned_ref[...] = owned_ref[...] + (sum_ref[:, lanes(own_base, half)] + sum_pair_ref[...])
        for k in range(len(near)):
            peer_z, copy = reduce_copy(k)
            guarded(peer_z < owners, copy.start)

    def start_rates(nothing):
        own = lanes(own_base, half)
        moment_ref[:, own] = moment_ref[:, own] + cross_ref[...]
        held = TILE * group // chunk
        for t in range(groups // TILE):
            out = jnp.zeros((modes, TILE), F32)
            for i in range(held):
                base = (t * held + i) * chunk
                sums = group_sums(moment_ref[:, base : base + chunk])
                out = jnp.where(lane // (TILE // held) == i, sums, out)
            rate_row_ref[mine, :, t * TILE : (t + 1) * TILE] = out
        for copy in rates_beside():
            copy.start()

    def start_gather(nothing):
        own_at = owned_at(mine, jnp.minimum(z, owners - 1))

        def finish_reduce():
            part = owned_ref[:, lanes(own_at, unit)]
            for k in range(len(near)):
                reduce_copy(k)[1].wait_recv()
                part = part + reduced_ref[k]
            gathered_ref[:, lanes(own_base + own_at, unit)] = part * norm
            for k in range(len(far)):
                gather_copy(k)[1].start()

        guarded(z < owners, finish_reduce)

    def start_along(nothing):
        for copy in rates_beside():
            copy.wait_recv()
        part = rate_row_ref[0]
        for i in range(1, rows):
            part = part + rate_row_ref[i]
        rate_seq_ref[me] = part
        for copy in rates_along():
            copy.start()

    events = {
        "total": send_total, "joint": send_joint, "take": take_total, "reduce": start_reduce, "gather": start_gather,
        "rates": start_rates, "along": start_along,
        "back": lambda k: to_back(k).wait_recv(), "sums": lambda k: sums_to_pair().start(),
    }

    def run_events(phase, j):
        for step, name, k in plan[phase]:
            @pl.when(j == step)
            def _():
                events[name](k)

    def lags(j, nothing):
        run_events("lags", j)
        base = base_of(j)
        here = lanes(base)
        x_hat_ref[:, here] = mul(waves_ref[0], twice(x_ref[:, here], 0))
        g_hat_ref[:, here] = mul(waves_ref[0], twice(g_ref[:, here], 0))
        for s in range(SUB):
            at = lanes(base + s * LANES, LANES)
            tile, shift = tile_of(base, s)
            upper = jnp.where(lane < length // 2, shift, shift + per_block // 2)
            pole, gap = [
                jnp.concatenate(
                    [pick_lanes(ref[:, tile], upper + g) for g in range(per_block // 2)], 0
                )
                for ref in (pole_ref, gap_ref)
            ]
            sums, moments = lag_block(
                modes, group, pole, gap, angle_ref[:, length // 2 :][:, :1],
                x_hat_ref[:, at], g_hat_ref[:, at],
            )
            sum_ref[:, at] = sums
            moment_ref[:, at] = -rates_ref[:, at] * res_ref[:, at] * moments
        return nothing

    for copy in late:
        copy.wait()
    weights_to_pair().start()
    send_total(0)
    lax.fori_loop(0, steps, lags, 0)

    order = plan["order"]

    def base_out(j):
        base = own_base
        for i, (own, k) in enumerate(order):
            base = jnp.where(j == i, (own_base if own else pair_base) + k * chunk, base)
        return base

    def outs(j, nothing):
        run_events("outs", j)
        base = base_out(j)
        for s in range(SUB):
            at = lanes(base + s * LANES, LANES)
            rate = rows_ref[lax.div(base, LANES) + s, 0:1, :]
            res = res_ref[:, at]
            pole = poles_ref[:, at]
            above = 1.0 + whole_ref[:, at]
            start_x = res * pole * (above * landed_ref[0, :, at] + state_ref[0, :, at])
            start_g = res * (above * landed_ref[1, :, at] + state_ref[1, :, at])
            y_hat, h_hat = hat_block(
                rate, waves_ref[3], angle_ref[:, : length // 2],
                x_hat_ref[:, at], g_hat_ref[:, at], res, start_x, start_g,
            )
            hat_ref[0, :, s * LANES : (s + 1) * LANES] = y_hat
            hat_ref[1, :, s * LANES : (s + 1) * LANES] = h_hat
        inverse = jnp.concatenate([waves_ref[1], waves_ref[2]], axis=0)
        here = lanes(base)
        y_ref[:, here] = fold_rows(mul(inverse, hat_ref[0])).astype(BF16)
        gs_ref[:, here] = fold_rows(mul(inverse, hat_ref[1])).astype(BF16)
        return nothing

    lax.fori_loop(0, steps, outs, 0)

    for k in range(len(far)):
        from_z, copy = gather_copy(k)
        guarded(from_z < owners, copy.wait_recv)
    for copy in spread_copies():
        copy.start()
    for copy in rates_along():
        copy.wait_recv()
    part = rate_seq_ref[0]
    for i in range(1, n):
        part = part + rate_seq_ref[i]
    grate_ref[...] = part * norm
    for copy in spread_copies():
        copy.wait_recv()

    for k in range(count):
        for copy in [to_pair(k), to_back(k), to_near(k)]:
            copy.wait_send()
        for wanted, copy in to_outer(k):
            pl.when(wanted)(copy.wait_send)
    sums_to_pair().wait_send()
    weights_to_pair().wait_send()
    for k in range(len(near)):
        peer_z, copy = reduce_copy(k)
        guarded(peer_z < owners, copy.wait_send)
    for k in range(len(far)):
        guarded(z < owners, gather_copy(k)[1].wait_send)
    for copy in rates_beside() + rates_along() + spread_copies():
        copy.wait_send()


def constants(length):
    half = length // 2
    omega = np.pi * (2.0 * np.arange(half) + 1.0) / length
    at = np.arange(length)
    forward = np.concatenate([np.cos(np.outer(omega, at)), -np.sin(np.outer(omega, at))], axis=0)
    parts = np.stack([2.0 * np.sin(omega / 2.0) ** 2, np.sin(omega)])
    angle = np.concatenate(
        [
            np.broadcast_to(parts[:, :, None], (2, half, 2 * half)),
            np.broadcast_to(np.tile(parts, (1, 2))[:, None], (2, 8, 2 * half)),
        ],
        axis=1,
    )
    return forward.astype(np.float32), (forward.T / half).astype(np.float32), angle.astype(np.float32)


def plan_of(count):
    last = 2 * count - 1
    own = [(True, k) for k in range(count)]
    pair = [(False, k) for k in range(count)]
    order = own[:2] + [v for both in zip(pair, own[2:] + [None] * 2) for v in both if v]
    lags = [(t, "total", k + 1) for k, t in enumerate([0, 1, 2])] + [(count, "sums", 0)]
    lags += [(t, "joint", k) for k, t in enumerate([3, 4, 5, 6])]
    lags += [(t, "take", k) for k, t in enumerate([7])]
    outs = [(t, "take", k + 1) for k, t in enumerate([0, 0, 1])]
    outs += [(1, "reduce", 0), (1, "rates", 0), (3, "gather", 0), (5, "along", 0)]
    outs += [(order.index(v), "back", v[1]) for v in pair]
    return {"lags": lags, "outs": outs, "order": order}


def leave_kernel(*refs):
    count = len(refs) // 2
    sems = refs[-1]
    copies = []
    for i, (source, target) in enumerate(zip(refs[:count], refs[count:])):
        copies.append(pltpu.make_async_copy(source, target, sems.at[i]))
    for copy in copies:
        copy.start()
    for copy in copies:
        copy.wait()


def leave(*arrays):
    return pl.pallas_call(
        leave_kernel,
        in_specs=[pl.BlockSpec(memory_space=pltpu.VMEM)] * len(arrays),
        out_specs=[pl.BlockSpec(memory_space=pltpu.HBM)] * len(arrays),
        out_shape=[pltpu.HBM(a.shape, a.dtype) for a in arrays],
        scratch_shapes=[pltpu.SemaphoreType.DMA((len(arrays),))],
        compiler_params=pltpu.CompilerParams(vmem_limit_bytes=4 * 1024 * 1024),
    )(*[pltpu.with_memory_space_constraint(a, pltpu.VMEM) for a in arrays])


def local(mesh_shape, signal, out_grad, residues, log_rates):
    batch_rows, length, channels = signal.shape
    modes, groups = log_rates.shape
    group = channels // groups
    n, rows = mesh_shape["seq"], mesh_shape["batch"]
    norm = 1.0 / (batch_rows * rows * length * n)
    forward, inverse, angle = constants(length)
    dft = np.asarray(forward).astype(jnp.bfloat16)
    dft = np.concatenate([dft, (forward - dft.astype(np.float32)).astype(jnp.bfloat16)], axis=1)
    inv_high = np.asarray(inverse).astype(jnp.bfloat16)
    inv_low = (inverse - inv_high.astype(np.float32)).astype(jnp.bfloat16)
    owner = np.arange(LANES)[None] // group == np.arange(LANES // group * modes)[:, None] // modes
    waves = np.stack(
        [dft] + [np.concatenate([v, v], axis=1) for v in (inv_high, inv_low)] + [owner.astype(jnp.bfloat16)]
    )
    half = channels // 2
    outer = n // 2
    count = half // (SUB * LANES)
    steps = 2 * count
    owners = min(outer, half // (rows * TILE))
    unit = half // (rows * owners)

    def dma(size):
        return pltpu.SemaphoreType.DMA((max(size, 1),))

    def vmem(*shape, dtype=F32):
        return pltpu.VMEM(shape, dtype)

    hbm_spec = pl.BlockSpec(memory_space=pltpu.HBM)
    vmem_spec = pl.BlockSpec(memory_space=pltpu.VMEM)
    links = [count, outer * count, count, 1, rows * outer - 1, rows * n - 1, rows - 1, n - 1, rows, 1, count]
    mixed, grads, res_sum, rate_sum = [], [], 0.0, 0.0
    for row in range(batch_rows):
        held = (
            signal[row], out_grad[row], residues, log_rates, jnp.asarray(waves), jnp.asarray(angle)
        )
        y, gs, part, rates = pl.pallas_call(
            functools.partial(whole_kernel, n, rows, norm, modes, group, owners, plan_of(count)),
            in_specs=[hbm_spec] * 6,
            out_specs=[vmem_spec] * 4,
            out_shape=[
                vmem(length, channels, dtype=BF16),
                vmem(length, channels, dtype=BF16),
                vmem(modes, channels),
                vmem(modes, groups),
            ],
            scratch_shapes=[
                vmem(length, channels, dtype=BF16),
                vmem(length, channels, dtype=BF16),
                vmem(modes, channels),
                vmem(modes, groups),
                vmem(*waves.shape, dtype=BF16),
                vmem(*angle.shape),
                vmem(modes, groups),
                vmem(modes, groups),
                vmem(modes, groups),
                vmem(modes, channels),
                vmem(modes, channels),
                vmem(modes, channels),
                vmem(modes, channels),
                vmem(channels // LANES, modes, TILE),
                vmem(2, modes, channels),
                vmem(2, modes, channels),
                vmem(length, channels),
                vmem(length, channels),
                vmem(2, 2 * length, SUB * LANES, dtype=BF16),
                vmem(modes, channels),
                vmem(modes, channels),
                vmem(modes, half),
                vmem(2, modes, half),
                vmem(2, modes, half),
                vmem(2, modes, half),
                vmem(modes, half),
                vmem(modes, half),
                vmem(outer // 2, modes, half),
                vmem(2, modes, half),
                vmem(2, modes, channels),
                vmem(modes, half),
                vmem(modes, half),
                vmem(max(rows * outer - 1, 1), modes, unit),
                vmem(rows, modes, groups),
                vmem(n, modes, groups),
                dma(2 * steps + 4),
            ]
            + [dma(size) for size in links for _ in range(2)],
            compiler_params=pltpu.CompilerParams(
                collective_id=0, has_side_effects=True, vmem_limit_bytes=32 * 1024 * 1024
            ),
        )(*[pltpu.with_memory_space_constraint(a, pltpu.HBM) for a in held])
        y, gs, part, rates = leave(y, gs, part, rates)
        mixed.append(y)
        grads.append(gs)
        res_sum = res_sum + part if row else part
        rate_sum = rate_sum + rates if row else rates
    return jnp.stack(mixed), jnp.stack(grads), res_sum, rate_sum


def solution(mesh):
    placed = (P("batch", "seq", None), P("batch", "seq", None), P(), P())
    return jax.shard_map(
        functools.partial(local, dict(mesh.shape)),
        mesh=mesh,
        in_specs=placed,
        out_specs=placed,
        check_vma=False,
    )
```

```python
import functools

import jax
import jax.numpy as jnp
import numpy as np
from jax import lax
from jax.experimental import pallas as pl
from jax.experimental.pallas import tpu as pltpu
from jax.sharding import PartitionSpec as P

LANES = 256
TILE = 128
SUB = 4
F32 = jnp.float32
BF16 = jnp.bfloat16
MESH = pl.DeviceIdType.MESH


def split(value):
    high = value.astype(BF16)
    return high, (value - high.astype(F32)).astype(BF16)


def mul(a, b):
    return jnp.dot(a, b, preferred_element_type=F32)


def twice(value, axis):
    return jnp.concatenate([value, value], axis=axis)


def own_rows(wide, modes, group):
    rows, lanes = wide.shape
    owner = lax.broadcasted_iota(jnp.int32, (modes, lanes), 1) // group
    out = wide[:modes]
    for g in range(1, rows // modes):
        out = jnp.where(owner == g, wide[g * modes : (g + 1) * modes], out)
    return out


def pick_lanes(tile, index):
    return jnp.take_along_axis(tile, index, axis=1, mode="promise_in_bounds")


def state_block(modes, group, rate, x, g):
    rows, length = rate.shape
    lane = lax.broadcasted_iota(jnp.int32, (rows, length), 1)
    at = lane.astype(F32)
    rising = jnp.exp(-rate * at)
    falling = pick_lanes(rising, length - 1 - lane)
    out = []
    for table, weight, values in ((falling, length - at, x), (rising, at, g)):
        left = jnp.concatenate([table, weight * table], axis=0)
        both = mul(jnp.concatenate(split(left), axis=1), twice(values, 0))
        out.append((own_rows(both[:rows], modes, group), own_rows(both[rows:], modes, group)))
    return out


def phi_of(pole, gap, angle):
    near = pole * angle[0]
    inverse = 1.0 / (gap * gap + (near + near))
    return (gap + near) * inverse, pole * angle[1] * inverse


def full(high, low):
    return jnp.concatenate([twice(high, 1), twice(low, 1)], axis=0)


def fold_rows(value):
    rows = value.shape[0] // 2
    return value[:rows] + value[rows:]


def lag_block(modes, group, pole, gap, angle, x_hat, g_hat):
    half = x_hat.shape[0] // 2
    r, i = phi_of(pole, gap, angle)
    lower = lax.broadcasted_iota(jnp.int32, r.shape, 1) < half
    terms = []
    for a, b in ((r, i), (r * r - i * i - r, 2.0 * r * i - i)):
        terms += [jnp.where(lower, a, pltpu.roll(b, half, 1)), jnp.where(lower, pltpu.roll(a, half, 1), b)]
    gm = 2 * r.shape[0]
    xr, xi = x_hat[:half], x_hat[half:]
    gr, gi = g_hat[:half], g_hat[half:]
    lag = jnp.concatenate([gr * xr + gi * xi, gr * xi - gi * xr], axis=0) * (1.0 / half)
    left = full(*split(jnp.concatenate(terms, axis=0)))
    wide = fold_rows(mul(left, jnp.concatenate(split(lag), axis=0)))
    return own_rows(wide[:gm], modes, group), own_rows(wide[gm:], modes, group)


def spread(narrow, mask):
    high, low = split(twice(narrow, 0))
    times = mask.shape[0] // high.shape[0]
    return jnp.concatenate(
        [jnp.concatenate([part] * times, axis=0) * mask for part in (high, low)], axis=0
    )


def hat_block(rate, mask, angle, x_hat, g_hat, res, start_x, start_g):
    half = x_hat.shape[0] // 2
    pole = jnp.exp(-rate)
    left = full(*split(jnp.concatenate(phi_of(pole, gap_of(rate), angle), axis=0)))
    right = jnp.concatenate([spread(v, mask) for v in (res, start_x, start_g)], axis=1)
    wide = fold_rows(mul(left, right))
    lanes = res.shape[1]
    (kr, ki), (cr, ci), (ar, ai) = [
        (wide[:half, at : at + lanes], wide[half:, at : at + lanes]) for at in (0, lanes, 2 * lanes)
    ]
    xr, xi = x_hat[:half], x_hat[half:]
    gr, gi = g_hat[:half], g_hat[half:]
    level = jnp.sum(start_g, axis=0, keepdims=True)
    y_hat = jnp.concatenate([kr * xr + ki * xi + cr, kr * xi - ki * xr - ci], axis=0)
    h_hat = jnp.concatenate([kr * gr - ki * gi + (level - ar), kr * gi + ki * gr - ai], axis=0)
    return jnp.concatenate(split(y_hat), axis=0), jnp.concatenate(split(h_hat), axis=0)


def gap_of(rate):
    gap = jnp.ones_like(rate)
    for k in range(7, 1, -1):
        gap = 1.0 - rate * gap * (1.0 / k)
    return rate * gap


def remote(source, target, sems, k, where):
    return pltpu.make_async_remote_copy(
        src_ref=source, dst_ref=target, send_sem=sems[0].at[k], recv_sem=sems[1].at[k],
        device_id=where, device_id_type=MESH,
    )


def whole_kernel(
    n, rows, norm, modes, group, owners, plan,
    x_hbm, g_hbm, res_hbm, log_hbm, waves_hbm, angle_hbm,
    y_ref, gs_ref, gathered_ref, grate_ref,
    x_ref, g_ref, res_ref, log_ref, waves_ref, angle_ref, decay_ref, pole_ref, gap_ref, rates_ref, poles_ref, whole_ref, fold_ref, rows_ref,
    state_ref, weighted_ref, x_hat_ref, g_hat_ref, hat_ref, sum_ref, moment_ref, cross_ref,
    pair_ref, weighted_pair_ref, total_ref, near_ref, joint_ref, outer_ref, back_ref, landed_ref, sum_pair_ref, owned_ref,
    reduced_ref, rate_row_ref, rate_seq_ref,
    in_sems, *sems,
):
    length, channels = x_ref.shape
    groups = log_ref.shape[1]
    half = channels // 2
    chunk = SUB * LANES
    count = half // chunk
    steps = 2 * count
    outer = n // 2
    me = lax.axis_index("seq")
    mine = lax.axis_index("batch")
    z, side = lax.div(me, 2), lax.rem(me, 2)
    two, odd, twos = lax.div(z, 2), lax.rem(z, 2), outer // 2
    own_base, pair_base = side * half, (1 - side) * half
    unit = half // (rows * owners)
    pairs = [(sems[2 * i], sems[2 * i + 1]) for i in range(len(sems) // 2)]
    partner = {"seq": me + 1 - 2 * side}

    def lanes(start, width=chunk):
        return pl.ds(pl.multiple_of(start, TILE), width)

    def base_of(j):
        return jnp.where(j < count, pair_base + j * chunk, own_base + (j - count) * chunk)

    def loads(j):
        here = lanes(base_of(j))
        return [
            pltpu.make_async_copy(x_hbm.at[:, here], x_ref.at[:, here], in_sems.at[j]),
            pltpu.make_async_copy(g_hbm.at[:, here], g_ref.at[:, here], in_sems.at[steps + j]),
        ]

    load_log = pltpu.make_async_copy(log_hbm, log_ref, in_sems.at[2 * steps])
    late = [
        pltpu.make_async_copy(source, target, in_sems.at[2 * steps + 1 + i])
        for i, (source, target) in enumerate(
            ((waves_hbm, waves_ref), (angle_hbm, angle_ref), (res_hbm, res_ref))
        )
    ]

    def to_pair(k):
        here = lanes(pair_base + k * chunk)
        return remote(
            state_ref.at[:, :, here], pair_ref.at[:, :, lanes(k * chunk)], pairs[0], k, partner
        )

    def weights_to_pair():
        return remote(
            weighted_ref.at[:, :, lanes(pair_base, half)], weighted_pair_ref, pairs[9], 0, partner
        )

    def to_near(k):
        here = lanes(k * chunk)
        return remote(
            total_ref.at[odd, :, here], near_ref.at[:, here], pairs[10], k,
            {"seq": 2 * (z + 1 - 2 * odd) + side},
        )

    def to_outer(k):
        here = lanes(k * chunk)
        out = []
        for q in range(twos):
            for m in range(2):
                wanted = jnp.where(odd == 1, q > two, q < two)
                out.append(
                    (
                        wanted,
                        pltpu.make_async_remote_copy(
                            src_ref=joint_ref.at[:, here], dst_ref=outer_ref.at[two, :, here],
                            send_sem=pairs[1][0].at[(2 * q + m) * count + k],
                            recv_sem=pairs[1][1].at[two * count + k],
                            device_id={"seq": 2 * (2 * q + m) + side}, device_id_type=MESH,
                        ),
                    )
                )
        return out

    def from_outer(k):
        here = lanes(k * chunk)
        return [
            (
                q != two,
                pltpu.make_async_remote_copy(
                    src_ref=joint_ref.at[:, here], dst_ref=outer_ref.at[q, :, here],
                    send_sem=pairs[1][0].at[2 * q * count + k], recv_sem=pairs[1][1].at[q * count + k],
                    device_id={"seq": 4 * q + side}, device_id_type=MESH,
                ),
            )
            for q in range(twos)
        ]

    def to_back(k):
        return remote(
            back_ref.at[:, :, lanes(k * chunk)], landed_ref.at[:, :, lanes(own_base + k * chunk)],
            pairs[2], k, partner,
        )

    def sums_to_pair():
        return remote(sum_ref.at[:, lanes(pair_base, half)], sum_pair_ref, pairs[3], 0, partner)

    def owned_at(q, zo):
        return q * (half // rows) + zo * unit

    def guarded(condition, action):
        if owners == outer:
            action()
        else:
            pl.when(condition)(action)

    near = [(q, i) for q in range(rows) for i in range(outer) if q or i]
    stride = 2 if rows % 2 == 0 else 1
    far = [(q, i) for q in range(0, rows, stride) for i in range(n) if q or i]
    known = [(q, i) for q in range(rows) for i in range(n) if (q or i) and (q % stride == 0 or i % 2 == 0)]

    def reduce_copy(k):
        q, i = near[k]
        peer_q, peer_z = lax.rem(mine + q, rows), lax.rem(z + i, outer)
        return peer_z, remote(
            owned_ref.at[:, lanes(owned_at(peer_q, jnp.minimum(peer_z, owners - 1)), unit)],
            reduced_ref.at[k], pairs[4], k, {"batch": peer_q, "seq": 2 * peer_z + side},
        )

    def gather_copy(k):
        q, i = far[k]
        here = lanes(own_base + owned_at(mine, jnp.minimum(z, owners - 1)), unit)
        return lax.div(lax.rem(me + n - i, n), 2), remote(
            gathered_ref.at[:, here], gathered_ref.at[:, here], pairs[5], k,
            {"batch": lax.rem(mine + q, rows), "seq": lax.rem(me + i, n)},
        )

    classes = [(q, i) for q in range(0, rows, 2) for i in range(2)] if stride == 2 else []

    def spread_copies():
        width = half // rows
        out = []
        for k, (q, i) in enumerate(classes):
            here = lanes(lax.rem(side + i, 2) * half + lax.rem(mine + rows - q, rows) * width, width)
            out.append(
                remote(
                    gathered_ref.at[:, here], gathered_ref.at[:, here], pairs[8], k,
                    {"batch": mine + 1 - 2 * lax.rem(mine, 2)},
                )
            )
        return out

    def rates_beside():
        return [
            remote(
                rate_row_ref.at[mine], rate_row_ref.at[mine], pairs[6], i - 1,
                {"batch": lax.rem(mine + i, rows)},
            )
            for i in range(1, rows)
        ]

    def rates_along():
        return [
            remote(
                rate_seq_ref.at[me], rate_seq_ref.at[me], pairs[7], i - 1,
                {"seq": lax.rem(me + i, n)},
            )
            for i in range(1, n)
        ]

    load_log.start()
    barrier = pltpu.get_barrier_semaphore()
    for copy in loads(0):
        copy.start()
    for q, i in known:
        pl.semaphore_signal(
            barrier, inc=1, device_id={"batch": lax.rem(mine + q, rows), "seq": lax.rem(me + i, n)},
            device_id_type=MESH,
        )
    for j in range(1, steps):
        for copy in loads(j):
            copy.start()
    for copy in late:
        copy.start()
    outer_ref[two] = jnp.zeros((modes, half), F32)

    load_log.wait()
    decay = jnp.exp(log_ref[...])
    decay_ref[...] = decay
    pole_ref[...] = jnp.exp(-decay)
    gap_ref[...] = gap_of(decay)
    per_block = LANES // group

    lane = lax.broadcasted_iota(jnp.int32, (modes, TILE), 1)
    sub = lax.broadcasted_iota(jnp.int32, (modes, TILE), 0)
    per_tile = TILE // group
    for k in range(channels // TILE):
        first = k * per_tile
        tile = decay_ref[:, first // TILE * TILE : (first // TILE + 1) * TILE]
        here = slice(k * TILE, (k + 1) * TILE)
        rate = pick_lanes(tile, lane // group + first % TILE)
        whole = jnp.exp(-rate * float(length))
        rates_ref[:, here] = rate
        poles_ref[:, here] = jnp.exp(-rate)
        whole_ref[:, here] = whole
        fold_ref[:, here] = 1.0 / (1.0 + whole)
    for b in range(channels // LANES):
        first = b * per_block
        tile = decay_ref[:, first // TILE * TILE : (first // TILE + 1) * TILE]
        taken = pick_lanes(tile, lane // modes + first % TILE)
        row = jnp.sum(jnp.where(lane % modes == sub, taken, 0.0), axis=0, keepdims=True)
        rows_ref[b] = jnp.broadcast_to(row, (modes, TILE))

    def tile_of(base, s):
        first = lax.div(base, group) + s * per_block
        return lanes(lax.div(first, TILE) * TILE, TILE), lax.rem(first, TILE)

    def states(j, nothing):
        base = base_of(j)
        for copy in loads(j):
            copy.wait()
        for s in range(SUB):
            at = lanes(base + s * LANES, LANES)
            tile, shift = tile_of(base, s)
            rate = jnp.concatenate(
                [
                    pick_lanes(decay_ref[:, tile], jnp.full((modes, TILE), shift + g))
                    for g in range(per_block)
                ],
                0,
            )
            (s_x, w_x), (s_g, w_g) = state_block(modes, group, rate, x_ref[:, at], g_ref[:, at])
            state_ref[0, :, at] = s_x
            state_ref[1, :, at] = s_g
            weighted_ref[0, :, at] = w_x
            weighted_ref[1, :, at] = w_g

        for k in range(count):
            @pl.when(j == k)
            def _():
                if k == 0:
                    pl.semaphore_wait(barrier, len(known))
                to_pair(k).start()

        return nothing

    lax.fori_loop(0, steps, states, 0)

    def both_of(k):
        at, here = lanes(own_base + k * chunk), lanes(k * chunk)
        first = side == 0
        ours, theirs = [state_ref[i, :, at] for i in (0, 1)], [pair_ref[i, :, here] for i in (0, 1)]
        a = [jnp.where(first, o, t) for o, t in zip(ours, theirs)]
        b = [jnp.where(first, t, o) for o, t in zip(ours, theirs)]
        return a, b, whole_ref[:, at], first, at, here

    def send_total(k):
        to_pair(k).wait_recv()
        a, b, whole, first, at, here = both_of(k)
        total_ref[0, :, here] = whole * a[0] + b[0]
        total_ref[1, :, here] = a[1] + whole * b[1]
        to_near(k).start()

    def send_joint(k):
        to_near(k).wait_recv()
        here = lanes(k * chunk)
        whole = whole_ref[:, lanes(own_base + k * chunk)]
        joint_ref[:, here] = whole * whole * near_ref[:, here] + total_ref[1 - odd, :, here]
        for wanted, copy in to_outer(k):
            pl.when(wanted)(copy.start)

    def take_total(k):
        for wanted, copy in from_outer(k):
            pl.when(wanted)(copy.wait_recv)
        a, b, whole, first, at, here = both_of(k)
        twofold = whole * whole
        fourfold = twofold * twofold
        carry = jnp.zeros_like(whole)
        adjoint = jnp.zeros_like(whole)
        for i in range(twos):
            carry = jnp.where(i < two, outer_ref[i, :, here] + fourfold * carry, carry)
            last = twos - 1 - i
            adjoint = jnp.where(last > two, outer_ref[last, :, here] + fourfold * adjoint, adjoint)
        beside = near_ref[:, here]
        carry = jnp.where(odd == 1, beside + twofold * carry, carry)
        adjoint = jnp.where(odd == 1, adjoint, beside + twofold * adjoint)
        carry_b = whole * carry + a[0]
        adjoint_a = whole * adjoint + b[1]
        back_ref[0, :, here] = jnp.where(first, carry_b, carry)
        back_ref[1, :, here] = jnp.where(first, adjoint, adjoint_a)
        to_back(k).start()
        landed_ref[0, :, at] = jnp.where(first, carry, carry_b)
        landed_ref[1, :, at] = jnp.where(first, adjoint_a, adjoint)
        if k == 0:
            weights_to_pair().wait_recv()
        ours = [weighted_ref[i, :, at] for i in (0, 1)]
        theirs = [weighted_pair_ref[i, :, here] for i in (0, 1)]
        cross, moments, fold = jnp.zeros_like(whole), jnp.zeros_like(whole), fold_ref[:, at]
        for (s_x, s_g), (w_x, w_g), into, back in (
            (a, [jnp.where(first, o, t) for o, t in zip(ours, theirs)], carry, adjoint_a),
            (b, [jnp.where(first, t, o) for o, t in zip(ours, theirs)], carry_b, adjoint),
        ):
            turned_x, turned_g = s_x * fold, s_g * fold
            into_all = into + turned_x
            cross += into_all * s_g
            moments += (into_all * w_g + (back + turned_g) * w_x) + float(length) * whole * (
                into * back - turned_x * turned_g
            )
        rate, pole = rates_ref[:, at], poles_ref[:, at]
        owned_ref[:, here] = pole * cross
        cross_ref[:, here] = -rate * res_ref[:, at] * pole * moments

    def group_sums(value):
        parts = [value[:, t * TILE : (t + 1) * TILE] for t in range(value.shape[1] // TILE)]
        many, shift = len(parts), 1
        while shift < group:
            if len(parts) > 1:
                low = (lane & shift) == 0
                parts = [
                    jnp.where(low, a, b) + pick_lanes(jnp.where(low, b, a), lane ^ shift)
                    for a, b in zip(parts[::2], parts[1::2])
                ]
            else:
                parts = [parts[0] + pick_lanes(parts[0], lane ^ shift)]
            shift *= 2
        return pick_lanes(parts[0], lane % per_tile * group + lane // per_tile % many)

    def start_reduce(nothing):
        sums_to_pair().wait_recv()
        owned_ref[...] = owned_ref[...] + (sum_ref[:, lanes(own_base, half)] + sum_pair_ref[...])
        for k in range(len(near)):
            peer_z, copy = reduce_copy(k)
            guarded(peer_z < owners, copy.start)

    def start_rates(nothing):
        own = lanes(own_base, half)
        moment_ref[:, own] = moment_ref[:, own] + cross_ref[...]
        held = TILE * group // chunk
        for t in range(groups // TILE):
            out = jnp.zeros((modes, TILE), F32)
            for i in range(held):
                base = (t * held + i) * chunk
                sums = group_sums(moment_ref[:, base : base + chunk])
                out = jnp.where(lane // (TILE // held) == i, sums, out)
            rate_row_ref[mine, :, t * TILE : (t + 1) * TILE] = out
        for copy in rates_beside():
            copy.start()

    def start_gather(nothing):
        own_at = owned_at(mine, jnp.minimum(z, owners - 1))

        def finish_reduce():
            part = owned_ref[:, lanes(own_at, unit)]
            for k in range(len(near)):
                reduce_copy(k)[1].wait_recv()
                part = part + reduced_ref[k]
            gathered_ref[:, lanes(own_base + own_at, unit)] = part * norm
            for k in range(len(far)):
                gather_copy(k)[1].start()

        guarded(z < owners, finish_reduce)

    def start_along(nothing):
        for copy in rates_beside():
            copy.wait_recv()
        part = rate_row_ref[0]
        for i in range(1, rows):
            part = part + rate_row_ref[i]
        rate_seq_ref[me] = part
        for copy in rates_along():
            copy.start()

    events = {
        "total": send_total, "joint": send_joint, "take": take_total, "reduce": start_reduce, "gather": start_gather,
        "rates": start_rates, "along": start_along,
        "back": lambda k: to_back(k).wait_recv(), "sums": lambda k: sums_to_pair().start(),
    }

    def run_events(phase, j):
        for step, name, k in plan[phase]:
            @pl.when(j == step)
            def _():
                events[name](k)

    def lags(j, nothing):
        run_events("lags", j)
        base = base_of(j)
        here = lanes(base)
        x_hat_ref[:, here] = mul(waves_ref[0], twice(x_ref[:, here], 0))
        g_hat_ref[:, here] = mul(waves_ref[0], twice(g_ref[:, here], 0))
        for s in range(SUB):
            at = lanes(base + s * LANES, LANES)
            tile, shift = tile_of(base, s)
            upper = jnp.where(lane < length // 2, shift, shift + per_block // 2)
            pole, gap = [
                jnp.concatenate(
                    [pick_lanes(ref[:, tile], upper + g) for g in range(per_block // 2)], 0
                )
                for ref in (pole_ref, gap_ref)
            ]
            sums, moments = lag_block(
                modes, group, pole, gap, angle_ref[:, length // 2 :][:, :1],
                x_hat_ref[:, at], g_hat_ref[:, at],
            )
            sum_ref[:, at] = sums
            moment_ref[:, at] = -rates_ref[:, at] * res_ref[:, at] * moments
        return nothing

    for copy in late:
        copy.wait()
    weights_to_pair().start()
    send_total(0)
    lax.fori_loop(0, steps, lags, 0)

    order = plan["order"]

    def base_out(j):
        base = own_base
        for i, (own, k) in enumerate(order):
            base = jnp.where(j == i, (own_base if own else pair_base) + k * chunk, base)
        return base

    def outs(j, nothing):
        run_events("outs", j)
        base = base_out(j)
        for s in range(SUB):
            at = lanes(base + s * LANES, LANES)
            rate = rows_ref[lax.div(base, LANES) + s, 0:1, :]
            res = res_ref[:, at]
            pole = poles_ref[:, at]
            above = 1.0 + whole_ref[:, at]
            start_x = res * pole * (above * landed_ref[0, :, at] + state_ref[0, :, at])
            start_g = res * (above * landed_ref[1, :, at] + state_ref[1, :, at])
            y_hat, h_hat = hat_block(
                rate, waves_ref[3], angle_ref[:, : length // 2],
                x_hat_ref[:, at], g_hat_ref[:, at], res, start_x, start_g,
            )
            hat_ref[0, :, s * LANES : (s + 1) * LANES] = y_hat
            hat_ref[1, :, s * LANES : (s + 1) * LANES] = h_hat
        inverse = jnp.concatenate([waves_ref[1], waves_ref[2]], axis=0)
        here = lanes(base)
        y_ref[:, here] = fold_rows(mul(inverse, hat_ref[0])).astype(BF16)
        gs_ref[:, here] = fold_rows(mul(inverse, hat_ref[1])).astype(BF16)
        return nothing

    lax.fori_loop(0, steps, outs, 0)

    for kind in classes or [None]:
        for k, (q, i) in enumerate(far):
            if kind in (None, (q, i % 2)):
                from_z, copy = gather_copy(k)
                guarded(from_z < owners, copy.wait_recv)
        if kind:
            spread_copies()[classes.index(kind)].start()
    for copy in rates_along():
        copy.wait_recv()
    part = rate_seq_ref[0]
    for i in range(1, n):
        part = part + rate_seq_ref[i]
    grate_ref[...] = part * norm
    for copy in spread_copies():
        copy.wait_recv()

    for k in range(count):
        for copy in [to_pair(k), to_back(k), to_near(k)]:
            copy.wait_send()
        for wanted, copy in to_outer(k):
            pl.when(wanted)(copy.wait_send)
    sums_to_pair().wait_send()
    weights_to_pair().wait_send()
    for k in range(len(near)):
        peer_z, copy = reduce_copy(k)
        guarded(peer_z < owners, copy.wait_send)
    for k in range(len(far)):
        guarded(z < owners, gather_copy(k)[1].wait_send)
    for copy in rates_beside() + rates_along() + spread_copies():
        copy.wait_send()


def constants(length):
    half = length // 2
    omega = np.pi * (2.0 * np.arange(half) + 1.0) / length
    at = np.arange(length)
    forward = np.concatenate([np.cos(np.outer(omega, at)), -np.sin(np.outer(omega, at))], axis=0)
    parts = np.stack([2.0 * np.sin(omega / 2.0) ** 2, np.sin(omega)])
    angle = np.concatenate(
        [
            np.broadcast_to(parts[:, :, None], (2, half, 2 * half)),
            np.broadcast_to(np.tile(parts, (1, 2))[:, None], (2, 8, 2 * half)),
        ],
        axis=1,
    )
    return forward.astype(np.float32), (forward.T / half).astype(np.float32), angle.astype(np.float32)


def plan_of(count):
    last = 2 * count - 1
    own = [(True, k) for k in range(count)]
    pair = [(False, k) for k in range(count)]
    order = own[:2] + [v for both in zip(pair, own[2:] + [None] * 2) for v in both if v]
    lags = [(t, "total", k + 1) for k, t in enumerate([0, 1, 2])] + [(count, "sums", 0)]
    lags += [(t, "joint", k) for k, t in enumerate([3, 4, 5, 6])]
    lags += [(t, "take", k) for k, t in enumerate([7])]
    outs = [(t, "take", k + 1) for k, t in enumerate([0, 0, 1])]
    outs += [(1, "reduce", 0), (1, "rates", 0), (3, "gather", 0), (5, "along", 0)]
    outs += [(order.index(v), "back", v[1]) for v in pair]
    return {"lags": lags, "outs": outs, "order": order}


def leave_kernel(*refs):
    count = len(refs) // 2
    sems = refs[-1]
    copies = []
    for i, (source, target) in enumerate(zip(refs[:count], refs[count:])):
        copies.append(pltpu.make_async_copy(source, target, sems.at[i]))
    for copy in copies:
        copy.start()
    for copy in copies:
        copy.wait()


def leave(*arrays):
    return pl.pallas_call(
        leave_kernel,
        in_specs=[pl.BlockSpec(memory_space=pltpu.VMEM)] * len(arrays),
        out_specs=[pl.BlockSpec(memory_space=pltpu.HBM)] * len(arrays),
        out_shape=[pltpu.HBM(a.shape, a.dtype) for a in arrays],
        scratch_shapes=[pltpu.SemaphoreType.DMA((len(arrays),))],
        compiler_params=pltpu.CompilerParams(vmem_limit_bytes=4 * 1024 * 1024),
    )(*[pltpu.with_memory_space_constraint(a, pltpu.VMEM) for a in arrays])


def local(mesh_shape, signal, out_grad, residues, log_rates):
    batch_rows, length, channels = signal.shape
    modes, groups = log_rates.shape
    group = channels // groups
    n, rows = mesh_shape["seq"], mesh_shape["batch"]
    norm = 1.0 / (batch_rows * rows * length * n)
    forward, inverse, angle = constants(length)
    dft = np.asarray(forward).astype(jnp.bfloat16)
    dft = np.concatenate([dft, (forward - dft.astype(np.float32)).astype(jnp.bfloat16)], axis=1)
    inv_high = np.asarray(inverse).astype(jnp.bfloat16)
    inv_low = (inverse - inv_high.astype(np.float32)).astype(jnp.bfloat16)
    owner = np.arange(LANES)[None] // group == np.arange(LANES // group * modes)[:, None] // modes
    waves = np.stack(
        [dft] + [np.concatenate([v, v], axis=1) for v in (inv_high, inv_low)] + [owner.astype(jnp.bfloat16)]
    )
    half = channels // 2
    outer = n // 2
    count = half // (SUB * LANES)
    steps = 2 * count
    owners = min(outer, half // (rows * TILE))
    unit = half // (rows * owners)

    def dma(size):
        return pltpu.SemaphoreType.DMA((max(size, 1),))

    def vmem(*shape, dtype=F32):
        return pltpu.VMEM(shape, dtype)

    hbm_spec = pl.BlockSpec(memory_space=pltpu.HBM)
    vmem_spec = pl.BlockSpec(memory_space=pltpu.VMEM)
    links = [count, outer * count, count, 1, rows * outer - 1, rows * n - 1, rows - 1, n - 1, rows, 1, count]
    mixed, grads, res_sum, rate_sum = [], [], 0.0, 0.0
    for row in range(batch_rows):
        held = (
            signal[row], out_grad[row], residues, log_rates, jnp.asarray(waves), jnp.asarray(angle)
        )
        y, gs, part, rates = pl.pallas_call(
            functools.partial(whole_kernel, n, rows, norm, modes, group, owners, plan_of(count)),
            in_specs=[hbm_spec] * 6,
            out_specs=[vmem_spec] * 4,
            out_shape=[
                vmem(length, channels, dtype=BF16),
                vmem(length, channels, dtype=BF16),
                vmem(modes, channels),
                vmem(modes, groups),
            ],
            scratch_shapes=[
                vmem(length, channels, dtype=BF16),
                vmem(length, channels, dtype=BF16),
                vmem(modes, channels),
                vmem(modes, groups),
                vmem(*waves.shape, dtype=BF16),
                vmem(*angle.shape),
                vmem(modes, groups),
                vmem(modes, groups),
                vmem(modes, groups),
                vmem(modes, channels),
                vmem(modes, channels),
                vmem(modes, channels),
                vmem(modes, channels),
                vmem(channels // LANES, modes, TILE),
                vmem(2, modes, channels),
                vmem(2, modes, channels),
                vmem(length, channels),
                vmem(length, channels),
                vmem(2, 2 * length, SUB * LANES, dtype=BF16),
                vmem(modes, channels),
                vmem(modes, channels),
                vmem(modes, half),
                vmem(2, modes, half),
                vmem(2, modes, half),
                vmem(2, modes, half),
                vmem(modes, half),
                vmem(modes, half),
                vmem(outer // 2, modes, half),
                vmem(2, modes, half),
                vmem(2, modes, channels),
                vmem(modes, half),
                vmem(modes, half),
                vmem(max(rows * outer - 1, 1), modes, unit),
                vmem(rows, modes, groups),
                vmem(n, modes, groups),
                dma(2 * steps + 4),
            ]
            + [dma(size) for size in links for _ in range(2)],
            compiler_params=pltpu.CompilerParams(
                collective_id=0, has_side_effects=True, vmem_limit_bytes=32 * 1024 * 1024
            ),
        )(*[pltpu.with_memory_space_constraint(a, pltpu.HBM) for a in held])
        y, gs, part, rates = leave(y, gs, part, rates)
        mixed.append(y)
        grads.append(gs)
        res_sum = res_sum + part if row else part
        rate_sum = rate_sum + rates if row else rates
    return jnp.stack(mixed), jnp.stack(grads), res_sum, rate_sum


def solution(mesh):
    placed = (P("batch", "seq", None), P("batch", "seq", None), P(), P())
    return jax.shard_map(
        functools.partial(local, dict(mesh.shape)),
        mesh=mesh,
        in_specs=placed,
        out_specs=placed,
        check_vma=False,
    )
```
